256 devices in a mesh: row: 64 (over z, x, core), col: 4 (over y).
Axes of the slice: x: 4, y: 4, z: 8, core: 2. Of those that a mesh axis runs over, the one named last changes fastest.
Arguments:
- tiles: bfloat16 [43008, 128, 128], P(('row', 'col')), may hold values from -0.0625 to 0.0625
- tile_slots: int32 [43008], P(('row', 'col')), may hold values from 0 to 383, as said below
- sketch: bfloat16 [24576, 512], P('col'), may hold values from -6 to 6
- row_sketch: bfloat16 [65536, 512], P(('row', 'col')), may hold values from -6 to 6
- subsketch: float32 [512, 128], replicated, may hold values from -0.25 to 0.25
- couplings: bfloat16 [256, 5, 128, 128], P(('row', 'col')), may hold values from -0.25 to 0.25, as said below
Outputs:
- leaf_basis: float32 [65536, 128], P(('row', 'col'))
- transfer: float32 [256, 5, 128, 128], P(('row', 'col'))
- top_samples: float32 [256, 128, 512], P(('row', 'col'))
The draws below stay inside these ranges and needn't reach their ends.
Inputs may be any that keep to these rules, and one draw needn't show every extreme that they name: `tile_slots`: the 168 slots of one device are distinct; slot v names row tile v // 48 and column tile v % 48. couplings[i, l] equals couplings[j, l] whenever i // 2 ** (l + 1) equals j // 2 ** (l + 1).
All inputs are finite; a program needn't handle non-finite values.
Results may differ from the reference program's by a relative error of at most 0.0003.
Values may be sent and summed in bfloat16 or wider, within the bound.
A program may use at most 128 MiB of HBM per device.

```python
import jax
import jax.numpy as jnp
from jax import lax

TILE = 128
LEAF = 256
S = 512
RANK = 128
LEVELS = 5
CTILES = 48
RTILES = 8
TILES = 168
LEAVES = 256
ROWS = 65536
COLS = 24576
N_ROW = 64
N_COL = 4


def draw_tile_slots(key, part):
    device_keys = jax.random.split(key, LEAVES)

    def one_device(device_key):
        return jax.random.permutation(device_key, RTILES * CTILES)[:TILES]
    return jax.vmap(one_device)(device_keys).reshape(LEAVES * TILES).astype(jnp.int32)


def draw_couplings(key, part):
    shape = (LEAVES, LEVELS, RANK, RANK)
    base = jnp.clip(jax.random.normal(key, shape, jnp.float32), -4.0, 4.0) * 0.0625
    leaf_ids = jnp.arange(LEAVES, dtype=jnp.int32)
    layers = []
    for tree_level in range(LEVELS):
        source = (leaf_ids // 2 ** (tree_level + 1) * 2 ** (tree_level + 1)).astype(jnp.int32)
        layers.append(jnp.take(base[:, tree_level], source, axis=0))
    return jnp.stack(layers, axis=1).astype(jnp.bfloat16)


def level_of(rng, dims, shards, least, high):
    level, own = 1.0, jax.random.fold_in(rng, 6)
    for axis_at, parts in shards:
        heights = jnp.exp(jax.random.uniform(jax.random.fold_in(own, axis_at), (parts,), jnp.float32, least / len(shards), high / len(shards)))
        level = level * jnp.repeat(heights, dims[axis_at] // parts).reshape([-1 if axis == axis_at else 1 for axis in range(len(dims))])
    return level


def centred(key, dims, spread, limit, shards=(), kind=jnp.bfloat16):
    drawn = spread * jax.random.normal(key, dims, jnp.float32)
    if shards:
        drawn = drawn * level_of(key, dims, shards, -0.22, 0.18)
    return jnp.clip(drawn, -limit, limit).astype(kind)


def setup_inputs(seed: int = 0) -> dict:
    streams_of = jax.random.split(jax.random.key(seed), 7)
    return {
        "tiles": centred(streams_of[0], (LEAVES * TILES, TILE, TILE), (TILE * TILES * N_COL // RTILES) ** -0.5, 0.0625, ((0, 256),)),
        "tile_slots": draw_tile_slots(jax.random.fold_in(streams_of[6], 71), 0),
        "sketch": centred(streams_of[2], (COLS, S), 1.0, 6.0, ((0, 4),)),
        "row_sketch": centred(streams_of[3], (ROWS, S), 1.0, 6.0, ((0, 256),)),
        "subsketch": centred(streams_of[4], (S, RANK), S ** -0.5, 0.25, (), jnp.float32),
        "couplings": draw_couplings(jax.random.fold_in(streams_of[6], 71), 0),
    }


def orthonormal(columns):
    gram = jnp.einsum('nr,nq->rq', columns, columns, precision=lax.Precision.HIGHEST)
    shift = 0.0001 * jnp.trace(gram) / gram.shape[0] + 1e-06
    lower = jnp.linalg.cholesky(gram + shift * jnp.eye(gram.shape[0], dtype=jnp.float32))
    basis_t = jax.scipy.linalg.solve_triangular(lower, columns.T, lower=True)
    return basis_t

def leaf_step(leaf_sample, leaf_sketch, subsketch):
    reduced = jnp.dot(leaf_sample, subsketch, precision=lax.Precision.HIGHEST)
    basis_t = orthonormal(reduced)
    proj_sample = jnp.dot(basis_t, leaf_sample, precision=lax.Precision.HIGHEST)
    proj_sketch = jnp.dot(basis_t, leaf_sketch.astype(jnp.float32), precision=lax.Precision.HIGHEST)
    return (basis_t.T, proj_sample, proj_sketch)

def merge_pair(low_sample, low_sketch, high_sample, high_sketch, coupling, subsketch):
    coup_f = coupling.astype(jnp.float32)
    low_part = low_sample - jnp.dot(coup_f, high_sketch, precision=lax.Precision.HIGHEST)
    high_part = high_sample - jnp.einsum('ji,js->is', coup_f, low_sketch, precision=lax.Precision.HIGHEST)
    stacked = jnp.concatenate([low_part, high_part], axis=0)
    stacked_sketch = jnp.concatenate([low_sketch, high_sketch], axis=0)
    reduced = jnp.dot(stacked, subsketch, precision=lax.Precision.HIGHEST)
    basis_t = orthonormal(reduced)
    new_sample = jnp.dot(basis_t, stacked, precision=lax.Precision.HIGHEST)
    new_sketch = jnp.dot(basis_t, stacked_sketch, precision=lax.Precision.HIGHEST)
    return (basis_t.T, new_sample, new_sketch)

def reference(tiles, tile_slots, sketch, row_sketch, subsketch, couplings):
    group_rows = RTILES * TILE
    tile_view = tiles.reshape(N_ROW, N_COL, TILES, TILE, TILE)
    slot_view = tile_slots.reshape(N_ROW, N_COL, TILES)
    sketch_view = sketch.reshape(N_COL, CTILES, TILE, S)

    def device_partial(dev_tiles, dev_slots, dev_sketch):
        picked = jnp.take(dev_sketch, dev_slots % CTILES, axis=0).astype(jnp.float32)
        product = jnp.einsum('tij,tjs->tis', dev_tiles.astype(jnp.float32), picked)
        summed = jax.ops.segment_sum(product, dev_slots // CTILES, num_segments=RTILES)
        return summed.reshape(group_rows, S)

    def group_sum(inputs):
        group_tiles, group_slots = inputs
        partials = jax.vmap(device_partial)(group_tiles, group_slots, sketch_view)
        return jnp.sum(partials, axis=0)
    samples = lax.map(group_sum, (tile_view, slot_view)).reshape(LEAVES, LEAF, S)
    leaf_rows = row_sketch.reshape(LEAVES, LEAF, S)
    bases, proj_sample, proj_sketch = jax.vmap(leaf_step, in_axes=(0, 0, None))(samples, leaf_rows, subsketch)
    leaf_basis = bases.reshape(LEAVES * LEAF, RANK)
    leaf_ids = jnp.arange(LEAVES, dtype=jnp.int32)
    blocks = []
    for tree_level in range(LEVELS):
        coupling = couplings[::2 ** (tree_level + 1), tree_level]
        parent_basis, proj_sample, proj_sketch = jax.vmap(merge_pair, in_axes=(0, 0, 0, 0, 0, None))(proj_sample[0::2], proj_sketch[0::2], proj_sample[1::2], proj_sketch[1::2], coupling, subsketch)
        node_count = parent_basis.shape[0]
        halves = parent_basis.reshape(node_count, 2, RANK, RANK)
        parent_ids = (leaf_ids // 2 ** (tree_level + 1)).astype(jnp.int32)
        half_ids = (leaf_ids // 2 ** tree_level % 2).astype(jnp.int32)
        blocks.append(halves[parent_ids, half_ids])
    transfer = jnp.stack(blocks, axis=1)
    top_samples = proj_sample[(leaf_ids // 2 ** LEVELS).astype(jnp.int32)]
    return (leaf_basis, transfer, top_samples)
```

```python
import functools

import jax
import jax.numpy as jnp
from jax import lax
from jax.experimental import pallas as pl
from jax.experimental.pallas import tpu as pltpu
from jax.sharding import PartitionSpec as P

LEVELS = 5
R = 128
F32 = jnp.float32
BF = jnp.bfloat16
HI = lax.Precision.HIGHEST
MESH = pl.DeviceIdType.MESH
LOW, HIGH = pl.ds(0, R), pl.ds(R, R)


def dot(a, b, ca=1, cb=0):
    return lax.dot_general(a, b, (((ca,), (cb,)), ((), ())), precision=HI, preferred_element_type=F32)


def dot16(a, b, ca=1, cb=0):
    return lax.dot_general(a, b, (((ca,), (cb,)), ((), ())), preferred_element_type=F32)


def split3(x):
    hi = x.astype(BF)
    rest = x - hi.astype(F32)
    mid = rest.astype(BF)
    return hi, mid, (rest - mid.astype(F32)).astype(BF)


def dot_bx(b, x, ca=1, cb=0):
    hi, mid, low = split3(x)
    return dot16(b, hi, ca, cb) + (dot16(b, mid, ca, cb) + dot16(b, low, ca, cb))


def dot_xb(x, b, ca=1, cb=0):
    hi, mid, low = split3(x)
    return dot16(hi, b, ca, cb) + (dot16(mid, b, ca, cb) + dot16(low, b, ca, cb))


def sample_kernel(step, slots_ref, tiles_ref, sketch_ref, sub_ref, y_ref, z_ref, dense, sk, present, tsem, ssem):
    tile_count = tiles_ref.shape[0]
    col_tiles = dense.shape[0]
    row_tiles = dense.shape[1] // R
    sketch_copy = pltpu.make_async_copy(sketch_ref, sk, ssem)
    sketch_copy.start()

    @pl.loop(0, present.shape[0], unroll=8)
    def _(v):
        present[v] = 0

    @pl.loop(0, tile_count, unroll=4)
    def _(t):
        v = slots_ref[t]
        present[v] = 1
        r = v // col_tiles
        rows = pl.ds(pl.multiple_of(r * R, R), R)
        pltpu.make_async_copy(tiles_ref.at[t], dense.at[v - r * col_tiles, rows, :], tsem).start()

    zero = jnp.zeros((R, R), BF)

    @pl.loop(0, present.shape[0])
    def _(v):
        @pl.when(present[v] == 0)
        def _():
            r = v // col_tiles
            dense[v - r * col_tiles, pl.ds(pl.multiple_of(r * R, R), R), :] = zero

    sketch_copy.wait()
    arrived = dense.at[pl.ds(0, tile_count // row_tiles)]
    pltpu.make_async_copy(arrived, arrived, tsem).wait()
    y_ref[...] = jnp.zeros_like(y_ref)

    @pl.loop(0, col_tiles // step)
    def _(p):
        lhs = jnp.concatenate([dense[p * step + i] for i in range(step)], axis=1)
        rhs = sk[pl.ds(pl.multiple_of(p * step * R, R), step * R), :]
        y_ref[...] += jnp.dot(lhs, rhs, preferred_element_type=F32)

    z_ref[...] = dot(y_ref[...], sub_ref[...])


def run_sample(tiles, slots, sketch, subsketch, row_tiles):
    col_tiles = sketch.shape[0] // R
    rows, width = row_tiles * R, sketch.shape[1]
    vmem = pl.BlockSpec(memory_space=pltpu.VMEM)
    hbm = pl.BlockSpec(memory_space=pl.ANY)
    return pl.pallas_call(
        functools.partial(sample_kernel, 8),
        out_shape=[jax.ShapeDtypeStruct((rows, width), F32), jax.ShapeDtypeStruct((rows, R), F32)],
        in_specs=[pl.BlockSpec(memory_space=pltpu.SMEM), hbm, hbm, vmem],
        out_specs=[vmem, vmem],
        scratch_shapes=[
            pltpu.VMEM((col_tiles, rows, R), BF),
            pltpu.VMEM(sketch.shape, BF),
            pltpu.SMEM((row_tiles * col_tiles,), jnp.int32),
            pltpu.SemaphoreType.DMA,
            pltpu.SemaphoreType.DMA,
        ],
        compiler_params=pltpu.CompilerParams(vmem_limit_bytes=60 * 2**20),
        name="sample",
    )(slots, tiles, sketch, subsketch)


def row_of(x, k):
    return jnp.broadcast_to(x[k : k + 1, :], x.shape)


def factor(ax, lt, middle):
    blocks = ax.shape[0]
    sub = lax.broadcasted_iota(jnp.int32, (8, 2 * R), 0)
    for j in range(blocks):
        if j == blocks // 2:
            middle()
        own = ax[j]
        cols = [jnp.broadcast_to(own[:, 8 * j + k : 8 * j + k + 1], (8, R)) for k in range(8)]
        d = [[row_of(cols[k], i) if i >= k else None for k in range(8)] for i in range(8)]
        rows = [row_of(own, k) for k in range(8)]
        inv, mult = [], [[None] * 8 for _ in range(8)]
        for k in range(8):
            inv.append(1.0 / d[k][k])
            for i in range(k + 1, 8):
                m = d[i][k] * inv[k]
                mult[i][k] = jnp.concatenate([m, m], axis=1)
                for i2 in range(i, 8):
                    d[i2][i] = d[i2][i] - d[i2][k] * m
                rows[i] = rows[i] - mult[i][k] * rows[k]
        out = rows[0]
        pivots = d[0][0]
        for k in range(1, 8):
            out = jnp.where(sub == k, rows[k], out)
            pivots = jnp.where(sub[:, :R] == k, d[k][k], pivots)
        scale = lax.rsqrt(pivots)
        lt[pl.ds(8 * j, 8), :] = out[:, :R] * scale
        ax[j, :, pl.ds(R, R)] = out[:, R:] * scale
        if j == blocks - 1:
            break
        q = [rows[k] * jnp.concatenate([inv[k], inv[k]], axis=1) for k in range(8)]
        for k in range(7, 0, -1):
            for i in range(k):
                q[i] = q[i] - mult[k][i] * q[k]
        for g in range(j + 1, blocks):
            rest = ax[g]
            terms = []
            for k in range(8):
                c = jnp.broadcast_to(rest[:, 8 * j + k : 8 * j + k + 1], (8, 2 * R))
                terms.append(c * q[k])
            while len(terms) > 1:
                terms = [terms[i] + terms[i + 1] for i in range(0, len(terms), 2)]
            ax[g] = rest - terms[0]


def tree_kernel(
    zpart, ypart, wrow, subsk, coup,
    leaf_out, trans_out, top_out,
    ax, lt, zb, wst, ub, comm, comm2, relay, fin, staged, sparts, vbuf, topbuf, cbuf, ybuf, ps,
    rs_send, rs_recv, ag_send, ag_recv, c_send, c_recv, c2_send, c2_recv, ysem,
):
    row, col = lax.axis_index("row"), lax.axis_index("col")
    position = row * 4 + col
    right, left = (col + 1) % 4, (col + 3) % 4
    across = (col + 2) % 4
    to_right, to_left = (row, right), (row, left)
    chip = row // 2
    core = row - chip * 2
    plane = chip // 4
    x = chip - plane * 4
    x_near = x + 1 - 2 * (x % 2)
    partners = [
        (row, col + 1 - 2 * (col % 2)),
        (row, 3 - col),
        (row + 1 - 2 * core, col),
        ((plane * 4 + x_near) * 2 + core, col),
        ((plane * 4 + 3 - x) * 2 + core, col),
    ]
    upper = [(position // 2**t) % 2 for t in range(LEVELS)]

    barrier = pltpu.get_barrier_semaphore()
    peers = [to_right, to_left] + partners[2:]
    for peer in peers:
        pl.semaphore_signal(barrier, inc=1, device_id=peer, device_id_type=MESH)
    pl.semaphore_wait(barrier, len(peers))

    def remote(src, dst, send, recv, peer):
        return pltpu.make_async_remote_copy(
            src_ref=src, dst_ref=dst, send_sem=send, recv_sem=recv, device_id=peer, device_id_type=MESH
        )

    def rs_copy(parts, n, i):
        src, dst, peer = [
            (parts.at[across, LOW], relay.at[n, 0], to_right),
            (parts.at[across, HIGH], relay.at[n, 1], to_left),
            (parts.at[right, HIGH], fin.at[n, 1], to_right),
            (parts.at[left, LOW], fin.at[n, 2], to_left),
            (staged.at[n, 0], fin.at[n, 0], to_right),
            (staged.at[n, 1], fin.at[n, 3], to_left),
        ][i]
        return remote(src, dst, rs_send.at[n, i], rs_recv.at[n, i], peer)

    def rs_first(parts, n):
        for i in range(4):
            rs_copy(parts, n, i).start()

    def rs_second(parts, n):
        rs_copy(parts, n, 0).wait_recv()
        staged[n, 0] = parts[right, LOW] + relay[n, 0]
        rs_copy(parts, n, 4).start()
        rs_copy(parts, n, 1).wait_recv()
        staged[n, 1] = parts[left, HIGH] + relay[n, 1]
        rs_copy(parts, n, 5).start()

    def rs_last(parts, n, out):
        for i in range(2, 6):
            rs_copy(parts, n, i).wait_recv()
        out[LOW] = parts[col, LOW] + (fin[n, 0] + fin[n, 2])
        out[HIGH] = parts[col, HIGH] + (fin[n, 1] + fin[n, 3])

    def rs_drain(parts, n):
        for i in range(6):
            rs_copy(parts, n, i).wait_send()

    def ag_copy(buf, n, i, receive=False):
        half = buf.shape[1] // 2
        first, second = pl.ds(0, half), pl.ds(half, half)
        if receive:
            ref = [buf.at[left], buf.at[right], buf.at[across, first], buf.at[across, second]][i]
        else:
            ref = [buf.at[col], buf.at[col], buf.at[left, first], buf.at[right, second]][i]
        return remote(ref, ref, ag_send.at[n, i], ag_recv.at[n, i], [to_right, to_left][i % 2])

    def ag_first(buf, n):
        for i in range(2):
            ag_copy(buf, n, i).start()

    def ag_second(buf, n):
        for i in range(2):
            ag_copy(buf, n, i, True).wait_recv()
            ag_copy(buf, n, i + 2).start()

    def ag_last(buf, n):
        for i in range(2, 4):
            ag_copy(buf, n, i, True).wait_recv()

    def ag_drain(buf, n):
        for i in range(4):
            ag_copy(buf, n, i).wait_send()

    def pair_copy(buf, base, t, send, recv):
        ref = buf.at[t - base, upper[t]]
        return remote(ref, ref, send.at[t - base], recv.at[t - base], partners[t])

    def pair_wait(buf, base, t, send, recv):
        ref = buf.at[t - base, 1 - upper[t]]
        remote(ref, ref, send.at[t - base], recv.at[t - base], partners[t]).wait_recv()

    y_copy = pltpu.make_async_copy(ypart, ybuf, ysem)
    y_copy.start()
    rs_first(zpart, 0)
    wst[...] = dot_bx(wrow[...], subsk[...])
    rs_second(zpart, 0)
    rs_last(zpart, 0, zb)

    def compose():
        def facing(t, other):
            b = coup[t]
            low = dot_bx(b, other)
            high = dot_bx(b, other, 0, 0)
            return jnp.where(upper[t] == 1, high, low)

        def halves(t):
            own = pl.ds(pl.multiple_of(upper[t] * R, R), R)
            other = pl.ds(pl.multiple_of((1 - upper[t]) * R, R), R)
            return ub[t + 1, own, :], ub[t + 1, other, :]

        own1, other1 = halves(0)
        own2, other2 = halves(1)
        v2 = dot(own1, own2)
        c2 = -(dot(facing(0, other1), own2) + dot(own1, facing(1, other2)))
        base = ub[0]
        v = dot(base, v2)
        vbuf[col] = v
        ag_first(vbuf, 0)
        c = dot(base, c2)
        w = wrow[...]
        ps[...] = dot_xb(c, w, 0, 0)
        pp = dot_xb(v, w, 0, 0)
        for k in range(4):
            sparts[k, HIGH] = pp[:, k * R : (k + 1) * R]

    def relay_bases():
        ag_second(vbuf, 0)

    def wide_parts():
        ag_last(vbuf, 0)
        y_copy.wait()

        @pl.loop(0, 4)
        def _(k):
            rows = pl.ds(pl.multiple_of(k * 2 * R, R), 2 * R)
            ps[...] += dot(vbuf[k], ybuf[rows, :], 0, 0)

        for k in range(4):
            sparts[k, LOW] = ps[:, k * R : (k + 1) * R]
        rs_first(sparts, 1)

    def relay_parts():
        rs_second(sparts, 1)

    def wide_start():
        rs_last(sparts, 1, comm2.at[0, upper[2]])
        pair_copy(comm2, 2, 2, c2_send, c2_recv).start()

    def wide_merge(t):
        pair_wait(comm2, 2, t, c2_send, c2_recv)
        low_p, high_p = comm2[t - 2, 0, HIGH], comm2[t - 2, 1, HIGH]
        low = comm2[t - 2, 0, LOW] - dot_bx(coup[t], high_p)
        high = comm2[t - 2, 1, LOW] - dot_bx(coup[t], low_p, 0, 0)
        u_low, u_high = ub[t + 1, LOW, :], ub[t + 1, HIGH, :]
        sample = dot(u_low, low, 0, 0) + dot(u_high, high, 0, 0)
        if t == LEVELS - 1:
            topbuf[col] = sample
            return
        comm2[t - 1, upper[t + 1], LOW] = sample
        comm2[t - 1, upper[t + 1], HIGH] = dot(u_low, low_p, 0, 0) + dot(u_high, high_p, 0, 0)
        pair_copy(comm2, 2, t + 1, c2_send, c2_recv).start()

    at_start = {4: relay_parts, 5: functools.partial(wide_merge, 3)}
    at_middle = {3: relay_bases, 4: wide_start}
    at_end = {2: compose, 3: wide_parts, 4: functools.partial(wide_merge, 2)}

    def place(table, t):
        for at, piece in table.items():
            pl.when(t == at)(piece)

    i0 = lax.broadcasted_iota(jnp.int32, (16, 8, R), 0) * 8 + lax.broadcasted_iota(jnp.int32, (16, 8, R), 1)
    eye = i0 == lax.broadcasted_iota(jnp.int32, (16, 8, R), 2)

    def stage(t, carry):
        for k in range(1, LEVELS + 1):
            @pl.when(t == k)
            def _():
                pair_wait(comm, 0, k - 1, c_send, c_recv)
                b = coup[k - 1]
                low_w, high_w = comm[k - 1, 0, HIGH], comm[k - 1, 1, HIGH]
                zb[LOW] = comm[k - 1, 0, LOW] - dot_bx(b, high_w)
                zb[HIGH] = comm[k - 1, 1, LOW] - dot_bx(b, low_w, 0, 0)
                wst[LOW] = low_w
                wst[HIGH] = high_w

        place(at_start, t)
        z = zb[...]
        gram = dot(z, z, 0, 0).reshape(16, 8, R)
        shift = 0.0001 * jnp.sum(z * z, keepdims=True) / R + 1e-06
        ax[:, :, pl.ds(0, R)] = gram + jnp.where(eye, shift.reshape(1, 1, 1), 0.0)
        ax[:, :, pl.ds(R, R)] = jnp.where(eye, 1.0, 0.0)
        factor(ax, lt, lambda: place(at_middle, t))
        linv = ax[:, :, pl.ds(R, R)].reshape(R, R)
        cross = dot(z, wst[...], 0, 0)
        for k in range(LEVELS):
            @pl.when(t == k)
            def _():
                comm[k, upper[k], LOW] = lt[...] - shift * linv
                comm[k, upper[k], HIGH] = dot(linv, cross)
                pair_copy(comm, 0, k, c_send, c_recv).start()

        u = dot(z, linv, 1, 1)
        ub[t] = u

        @pl.when(t == 0)
        def _():
            leaf_out[...] = u

        for k in range(LEVELS):
            @pl.when(t == k + 1)
            def _():
                trans_out[k] = ub[t, pl.ds(pl.multiple_of(upper[k] * R, R), R), :]

        place(at_end, t)
        return carry

    lax.fori_loop(0, LEVELS + 1, stage, 0)
    wide_merge(LEVELS - 1)
    ag_first(topbuf, 1)
    ag_second(topbuf, 1)
    ag_last(topbuf, 1)
    for k in range(4):
        top_out[:, pl.ds(k * R, R)] = topbuf[k]

    rs_drain(zpart, 0)
    rs_drain(sparts, 1)
    ag_drain(vbuf, 0)
    ag_drain(topbuf, 1)
    for t in range(LEVELS):
        pair_copy(comm, 0, t, c_send, c_recv).wait_send()
    for t in range(2, LEVELS):
        pair_copy(comm2, 2, t, c2_send, c2_recv).wait_send()


def run_tree(zpart, ypart, wrow, subsketch, couplings):
    vmem = pl.BlockSpec(memory_space=pltpu.VMEM)
    hbm = pl.BlockSpec(memory_space=pl.ANY)
    dma = pltpu.SemaphoreType.DMA
    width = ypart.shape[1]

    def f32(*shape):
        return pltpu.VMEM(shape, F32)

    return pl.pallas_call(
        tree_kernel,
        out_shape=[
            jax.ShapeDtypeStruct((2 * R, R), F32),
            jax.ShapeDtypeStruct((LEVELS, R, R), F32),
            jax.ShapeDtypeStruct((R, width), F32),
        ],
        in_specs=[vmem, hbm, vmem, vmem, vmem],
        out_specs=[vmem, vmem, vmem],
        scratch_shapes=[
            f32(16, 8, 2 * R), f32(R, R), f32(2 * R, R), f32(2 * R, R), f32(LEVELS + 1, 2 * R, R),
            f32(LEVELS, 2, 2 * R, R), f32(3, 2, 2 * R, R), f32(2, 2, R, R), f32(2, 4, R, R), f32(2, 2, R, R),
            f32(4, 2 * R, R), f32(4, 2 * R, R), f32(4, R, R), f32(2 * R, R), f32(*ypart.shape), f32(R, width),
            dma((2, 6)), dma((2, 6)), dma((2, 4)), dma((2, 4)), dma((LEVELS,)), dma((LEVELS,)), dma((3,)), dma((3,)), dma,
        ],
        compiler_params=pltpu.CompilerParams(
            collective_id=0, has_side_effects=True, vmem_limit_bytes=48 * 2**20
        ),
        name="tree",
    )(zpart, ypart, wrow, subsketch, couplings)


def per_device(tiles, tile_slots, sketch, row_sketch, subsketch, couplings):
    row_tiles = row_sketch.shape[0] * lax.axis_size("col") // R
    ypart, zpart = run_sample(tiles, tile_slots, sketch, subsketch, row_tiles)
    leaf_basis, transfer, top = run_tree(
        zpart.reshape(4, 2 * R, R), ypart, row_sketch, subsketch, couplings[0]
    )
    return leaf_basis, transfer[None], top[None]


def solution(mesh):
    return jax.shard_map(
        per_device,
        mesh=mesh,
        in_specs=(
            P(("row", "col"), None, None),
            P(("row", "col")),
            P("col", None),
            P(("row", "col"), None),
            P(),
            P(("row", "col"), None, None, None),
        ),
        out_specs=(
            P(("row", "col"), None),
            P(("row", "col"), None, None, None),
            P(("row", "col"), None, None),
        ),
        check_vma=False,
    )
```

```python
import functools

import jax
import jax.numpy as jnp
from jax import lax
from jax.experimental import pallas as pl
from jax.experimental.pallas import tpu as pltpu
from jax.sharding import PartitionSpec as P

LEVELS = 5
R = 128
F32 = jnp.float32
BF = jnp.bfloat16
HI = lax.Precision.HIGHEST
MESH = pl.DeviceIdType.MESH
LOW, HIGH = pl.ds(0, R), pl.ds(R, R)


def dot(a, b, ca=1, cb=0):
    return lax.dot_general(a, b, (((ca,), (cb,)), ((), ())), precision=HI, preferred_element_type=F32)


def dot16(a, b, ca=1, cb=0):
    return lax.dot_general(a, b, (((ca,), (cb,)), ((), ())), preferred_element_type=F32)


def split3(x):
    hi = x.astype(BF)
    rest = x - hi.astype(F32)
    mid = rest.astype(BF)
    return hi, mid, (rest - mid.astype(F32)).astype(BF)


def dot_bx(b, x, ca=1, cb=0):
    hi, mid, low = split3(x)
    return dot16(b, hi, ca, cb) + (dot16(b, mid, ca, cb) + dot16(b, low, ca, cb))


def dot_xb(x, b, ca=1, cb=0):
    hi, mid, low = split3(x)
    return dot16(hi, b, ca, cb) + (dot16(mid, b, ca, cb) + dot16(low, b, ca, cb))


def row_of(x, k):
    return jnp.broadcast_to(x[k : k + 1, :], x.shape)


def factor(ax, lt, middle):
    blocks = ax.shape[0]
    sub = lax.broadcasted_iota(jnp.int32, (8, 2 * R), 0)
    for j in range(blocks):
        if j == blocks // 2:
            middle()
        own = ax[j] if j == 0 else following
        cols = [jnp.broadcast_to(own[:, 8 * j + k : 8 * j + k + 1], (8, R)) for k in range(8)]
        d = [[row_of(cols[k], i) if i >= k else None for k in range(8)] for i in range(8)]
        rows = [row_of(own, k) for k in range(8)]
        inv, mult = [], [[None] * 8 for _ in range(8)]
        for k in range(8):
            inv.append(1.0 / d[k][k])
            for i in range(k + 1, 8):
                m = d[i][k] * inv[k]
                mult[i][k] = jnp.concatenate([m, m], axis=1)
                for i2 in range(i, 8):
                    d[i2][i] = d[i2][i] - d[i2][k] * m
                rows[i] = rows[i] - mult[i][k] * rows[k]
        out = rows[0]
        pivots = d[0][0]
        for k in range(1, 8):
            out = jnp.where(sub == k, rows[k], out)
            pivots = jnp.where(sub[:, :R] == k, d[k][k], pivots)
        scale = lax.rsqrt(pivots)
        lt[pl.ds(8 * j, 8), :] = out[:, :R] * scale
        ax[j, :, pl.ds(R, R)] = out[:, R:] * scale
        if j == blocks - 1:
            break
        q = [rows[k] * jnp.concatenate([inv[k], inv[k]], axis=1) for k in range(8)]
        for k in range(7, 0, -1):
            for i in range(k):
                q[i] = q[i] - mult[k][i] * q[k]
        for g in range(j + 1, blocks):
            rest = ax[g]
            terms = []
            for k in range(8):
                c = jnp.broadcast_to(rest[:, 8 * j + k : 8 * j + k + 1], (8, 2 * R))
                terms.append(c * q[k])
            while len(terms) > 1:
                terms = [terms[i] + terms[i + 1] for i in range(0, len(terms), 2)]
            rest = rest - terms[0]
            if g == j + 1:
                following = rest
            else:
                ax[g] = rest


def tree_kernel(
    slots, tiles_hbm, sketch_hbm, wrow_hbm, subsk_hbm, coup_hbm,
    leaf_out, trans_out, top_out,
    tiles, sketch, wrow, subsk, coup, slot_pad, index_row, index,
    ax, lt, zb, wst, ub, comm, comm2, relay, fin, staged, zparts, sparts, vbuf, topbuf, ybuf, ps,
    rs_send, rs_recv, ag_send, ag_recv, c_send, c_recv, c2_send, c2_recv, t_sem, k_sem, i_sem, n_sem,
):
    tile_count = tiles_hbm.shape[0]
    col_tiles = sketch_hbm.shape[0] // R

    def load(src, dst, sem):
        copy = pltpu.make_async_copy(src, dst, sem)
        copy.start()
        return copy

    small = [
        load(src, dst, i_sem.at[i])
        for i, (src, dst) in enumerate([(wrow_hbm, wrow), (subsk_hbm, subsk)])
    ]
    per = tile_count // t_sem.shape[0]
    tile_copies = [
        load(tiles_hbm.at[pl.ds(i * per, per)], tiles.at[pl.ds(i * per, per)], t_sem.at[i])
        for i in range(t_sem.shape[0])
    ]
    chunk = sketch_hbm.shape[0] // k_sem.shape[0]
    for i in range(k_sem.shape[0]):
        load(sketch_hbm.at[pl.ds(i * chunk, chunk)], sketch.at[pl.ds(i * chunk, chunk)], k_sem.at[i])
    small.append(load(coup_hbm, coup, i_sem.at[2]))

    slot_pad[...] = jnp.full_like(slot_pad, -1)
    slot_pad[pl.ds(0, 1), pl.ds(0, tile_count)] = slots[...]
    by_tile = jnp.broadcast_to(slot_pad[pl.ds(0, 1), :], (R, slot_pad.shape[1])).T
    which = jnp.minimum(lax.broadcasted_iota(jnp.int32, by_tile.shape, 0), tile_count)
    lane = lax.broadcasted_iota(jnp.int32, by_tile.shape, 1)
    for i in range(index_row.shape[1] // R):
        found = jnp.where(by_tile == lane + i * R, which, tile_count)
        index_row[:, pl.ds(i * R, R)] = jnp.min(found, axis=0, keepdims=True)
    index_copy = load(index_row, index, n_sem)
    tiles[tile_count] = jnp.zeros((R, R), BF)

    row, col = lax.axis_index("row"), lax.axis_index("col")
    position = row * 4 + col
    right, left = (col + 1) % 4, (col + 3) % 4
    across = (col + 2) % 4
    to_right, to_left = (row, right), (row, left)
    chip = row // 2
    core = row - chip * 2
    plane = chip // 4
    x = chip - plane * 4
    x_near = x + 1 - 2 * (x % 2)
    partners = [
        (row, col + 1 - 2 * (col % 2)),
        (row, 3 - col),
        (row + 1 - 2 * core, col),
        ((plane * 4 + x_near) * 2 + core, col),
        ((plane * 4 + 3 - x) * 2 + core, col),
    ]
    upper = [(position // 2**t) % 2 for t in range(LEVELS)]

    barrier = pltpu.get_barrier_semaphore()
    peers = [to_right, to_left] + partners[2:]
    for peer in peers:
        pl.semaphore_signal(barrier, inc=1, device_id=peer, device_id_type=MESH)
    pl.semaphore_wait(barrier, len(peers))

    def remote(src, dst, send, recv, peer):
        return pltpu.make_async_remote_copy(
            src_ref=src, dst_ref=dst, send_sem=send, recv_sem=recv, device_id=peer, device_id_type=MESH
        )

    def rs_copy(parts, n, i):
        src, dst, peer = [
            (parts.at[across, LOW], relay.at[n, 0], to_right),
            (parts.at[across, HIGH], relay.at[n, 1], to_left),
            (parts.at[right, HIGH], fin.at[n, 1], to_right),
            (parts.at[left, LOW], fin.at[n, 2], to_left),
            (staged.at[n, 0], fin.at[n, 0], to_right),
            (staged.at[n, 1], fin.at[n, 3], to_left),
        ][i]
        return remote(src, dst, rs_send.at[n, i], rs_recv.at[n, i], peer)

    def rs_first(parts, n):
        for i in range(4):
            rs_copy(parts, n, i).start()

    def rs_second(parts, n):
        rs_copy(parts, n, 0).wait_recv()
        staged[n, 0] = parts[right, LOW] + relay[n, 0]
        rs_copy(parts, n, 4).start()
        rs_copy(parts, n, 1).wait_recv()
        staged[n, 1] = parts[left, HIGH] + relay[n, 1]
        rs_copy(parts, n, 5).start()

    def rs_last(parts, n, out):
        for i in range(2, 6):
            rs_copy(parts, n, i).wait_recv()
        out[LOW] = parts[col, LOW] + (fin[n, 0] + fin[n, 2])
        out[HIGH] = parts[col, HIGH] + (fin[n, 1] + fin[n, 3])

    def rs_drain(parts, n):
        for i in range(6):
            rs_copy(parts, n, i).wait_send()

    def ag_copy(buf, n, i, receive=False):
        half = buf.shape[1] // 2
        first, second = pl.ds(0, half), pl.ds(half, half)
        if receive:
            ref = [buf.at[left], buf.at[right], buf.at[across, first], buf.at[across, second]][i]
        else:
            ref = [buf.at[col], buf.at[col], buf.at[left, first], buf.at[right, second]][i]
        return remote(ref, ref, ag_send.at[n, i], ag_recv.at[n, i], [to_right, to_left][i % 2])

    def ag_first(buf, n):
        for i in range(2):
            ag_copy(buf, n, i).start()

    def ag_second(buf, n):
        for i in range(2):
            ag_copy(buf, n, i, True).wait_recv()
            ag_copy(buf, n, i + 2).start()

    def ag_last(buf, n):
        for i in range(2, 4):
            ag_copy(buf, n, i, True).wait_recv()

    def ag_drain(buf, n):
        for i in range(4):
            ag_copy(buf, n, i).wait_send()

    def pair_copy(buf, base, t, send, recv):
        ref = buf.at[t - base, upper[t]]
        return remote(ref, ref, send.at[t - base], recv.at[t - base], partners[t])

    def pair_wait(buf, base, t, send, recv):
        ref = buf.at[t - base, 1 - upper[t]]
        remote(ref, ref, send.at[t - base], recv.at[t - base], partners[t]).wait_recv()

    def leaf_rows(leaf):
        return pl.ds(pl.multiple_of(leaf * 2 * R, R), 2 * R)

    def block_rows(leaf, first, count):
        return jnp.concatenate(
            [
                jnp.concatenate([tiles[index[0, (2 * leaf + i) * col_tiles + first + k]] for k in range(count)], axis=1)
                for i in range(2)
            ],
            axis=0,
        )

    def partial_samples(leaves, count, arriving):
        for leaf in leaves:
            ybuf[leaf_rows(leaf), :] = jnp.zeros((2 * R, ybuf.shape[1]), F32)

        @pl.loop(0, col_tiles // count)
        def _(p):
            rows = pl.ds(pl.multiple_of(p * count * R, R), count * R)
            if arriving:
                pltpu.make_async_copy(sketch_hbm.at[rows], sketch.at[rows], k_sem.at[p]).wait()
            lhs = jnp.concatenate([block_rows(leaf, p * count, count) for leaf in leaves], axis=0)
            product = dot16(lhs, sketch[rows, :])
            for i, leaf in enumerate(leaves):
                ybuf[leaf_rows(leaf), :] += product[i * 2 * R : (i + 1) * 2 * R]

        for leaf in leaves:
            zparts[leaf] = dot(ybuf[leaf_rows(leaf), :], subsk[...])

    small[0].wait()
    small[1].wait()
    wst[...] = dot_bx(wrow[...], subsk[...])
    index_copy.wait()
    for copy in tile_copies:
        copy.wait()
    partial_samples([across, right], col_tiles // k_sem.shape[0], True)
    for i in range(3):
        rs_copy(zparts, 0, i).start()
    partial_samples([left], 8, False)
    rs_copy(zparts, 0, 3).start()
    rs_second(zparts, 0)
    partial_samples([col], 8, False)
    small[2].wait()
    rs_last(zparts, 0, zb)

    def compose():
        def facing(t, other):
            b = coup[t]
            low = dot_bx(b, other)
            high = dot_bx(b, other, 0, 0)
            return jnp.where(upper[t] == 1, high, low)

        def halves(t):
            own = pl.ds(pl.multiple_of(upper[t] * R, R), R)
            other = pl.ds(pl.multiple_of((1 - upper[t]) * R, R), R)
            return ub[t + 1, own, :], ub[t + 1, other, :]

        own1, other1 = halves(0)
        own2, other2 = halves(1)
        v2 = dot(own1, own2)
        c2 = -(dot(facing(0, other1), own2) + dot(own1, facing(1, other2)))
        base = ub[0]
        v = dot(base, v2)
        vbuf[col] = v
        ag_first(vbuf, 0)
        c = dot(base, c2)
        w = wrow[...]
        ps[...] = dot_xb(c, w, 0, 0)
        pp = dot_xb(v, w, 0, 0)
        for k in range(4):
            sparts[k, HIGH] = pp[:, k * R : (k + 1) * R]

    def relay_bases():
        ag_second(vbuf, 0)

    def wide_parts():
        ag_last(vbuf, 0)

        @pl.loop(0, 4)
        def _(k):
            rows = pl.ds(pl.multiple_of(k * 2 * R, R), 2 * R)
            ps[...] += dot(vbuf[k], ybuf[rows, :], 0, 0)

        for k in range(4):
            sparts[k, LOW] = ps[:, k * R : (k + 1) * R]
        rs_first(sparts, 1)

    def relay_parts():
        rs_second(sparts, 1)

    def wide_start():
        rs_last(sparts, 1, comm2.at[0, upper[2]])
        pair_copy(comm2, 2, 2, c2_send, c2_recv).start()

    def wide_merge(t):
        pair_wait(comm2, 2, t, c2_send, c2_recv)
        low_p, high_p = comm2[t - 2, 0, HIGH], comm2[t - 2, 1, HIGH]
        low = comm2[t - 2, 0, LOW] - dot_bx(coup[t], high_p)
        high = comm2[t - 2, 1, LOW] - dot_bx(coup[t], low_p, 0, 0)
        u_low, u_high = ub[t + 1, LOW, :], ub[t + 1, HIGH, :]
        sample = dot(u_low, low, 0, 0) + dot(u_high, high, 0, 0)
        if t == LEVELS - 1:
            topbuf[col] = sample
            return
        comm2[t - 1, upper[t + 1], LOW] = sample
        comm2[t - 1, upper[t + 1], HIGH] = dot(u_low, low_p, 0, 0) + dot(u_high, high_p, 0, 0)
        pair_copy(comm2, 2, t + 1, c2_send, c2_recv).start()

    at_start = {4: relay_parts, 5: functools.partial(wide_merge, 3)}
    at_middle = {3: relay_bases, 4: wide_start}
    at_end = {2: compose, 3: wide_parts, 4: functools.partial(wide_merge, 2)}

    def place(table, t):
        for at, piece in table.items():
            pl.when(t == at)(piece)

    i0 = lax.broadcasted_iota(jnp.int32, (16, 8, R), 0) * 8 + lax.broadcasted_iota(jnp.int32, (16, 8, R), 1)
    eye = i0 == lax.broadcasted_iota(jnp.int32, (16, 8, R), 2)

    def stage(t, carry):
        for k in range(1, LEVELS + 1):
            @pl.when(t == k)
            def _():
                pair_wait(comm, 0, k - 1, c_send, c_recv)
                b = coup[k - 1]
                low_w, high_w = comm[k - 1, 0, HIGH], comm[k - 1, 1, HIGH]
                zb[LOW] = comm[k - 1, 0, LOW] - dot_bx(b, high_w)
                zb[HIGH] = comm[k - 1, 1, LOW] - dot_bx(b, low_w, 0, 0)
                wst[LOW] = low_w
                wst[HIGH] = high_w

        place(at_start, t)
        z = zb[...]
        gram = dot(z, z, 0, 0).reshape(16, 8, R)
        shift = 0.0001 * jnp.sum(z * z, keepdims=True) / R + 1e-06
        ax[:, :, pl.ds(0, R)] = gram + jnp.where(eye, shift.reshape(1, 1, 1), 0.0)
        ax[:, :, pl.ds(R, R)] = jnp.where(eye, 1.0, 0.0)
        factor(ax, lt, lambda: place(at_middle, t))
        linv = ax[:, :, pl.ds(R, R)].reshape(R, R)
        cross = dot(z, wst[...], 0, 0)
        for k in range(LEVELS):
            @pl.when(t == k)
            def _():
                comm[k, upper[k], LOW] = lt[...] - shift * linv
                comm[k, upper[k], HIGH] = dot(linv, cross)
                pair_copy(comm, 0, k, c_send, c_recv).start()

        u = dot(z, linv, 1, 1)
        ub[t] = u

        @pl.when(t == 0)
        def _():
            leaf_out[...] = u

        for k in range(LEVELS):
            @pl.when(t == k + 1)
            def _():
                trans_out[k] = ub[t, pl.ds(pl.multiple_of(upper[k] * R, R), R), :]

        place(at_end, t)
        return carry

    lax.fori_loop(0, LEVELS + 1, stage, 0)
    wide_merge(LEVELS - 1)
    ag_first(topbuf, 1)
    ag_second(topbuf, 1)
    ag_last(topbuf, 1)
    for k in range(4):
        top_out[:, pl.ds(k * R, R)] = topbuf[k]

    rs_drain(zparts, 0)
    rs_drain(sparts, 1)
    ag_drain(vbuf, 0)
    ag_drain(topbuf, 1)
    for t in range(LEVELS):
        pair_copy(comm, 0, t, c_send, c_recv).wait_send()
    for t in range(2, LEVELS):
        pair_copy(comm2, 2, t, c2_send, c2_recv).wait_send()


def run_tree(slots, tiles, sketch, wrow, subsketch, couplings):
    vmem = pl.BlockSpec(memory_space=pltpu.VMEM)
    hbm = pl.BlockSpec(memory_space=pltpu.HBM)
    dma = pltpu.SemaphoreType.DMA
    tile_count = tiles.shape[0]
    depth, width = sketch.shape
    slot_count = 8 * depth // R

    def f32(*shape):
        return pltpu.VMEM(shape, F32)

    return pl.pallas_call(
        tree_kernel,
        out_shape=[
            jax.ShapeDtypeStruct((2 * R, R), F32),
            jax.ShapeDtypeStruct((LEVELS, R, R), F32),
            jax.ShapeDtypeStruct((R, width), F32),
        ],
        in_specs=[vmem, hbm, hbm, hbm, hbm, hbm],
        out_specs=[vmem, vmem, vmem],
        scratch_shapes=[
            pltpu.VMEM((tile_count + 1, R, R), BF), pltpu.VMEM((depth, width), BF), pltpu.VMEM(wrow.shape, BF),
            f32(width, R), pltpu.VMEM(couplings.shape, BF), pltpu.VMEM((1, 2 * R), jnp.int32),
            pltpu.VMEM((1, slot_count), jnp.int32), pltpu.SMEM((1, slot_count), jnp.int32),
            f32(16, 8, 2 * R), f32(R, R), f32(2 * R, R), f32(2 * R, R), f32(LEVELS + 1, 2 * R, R),
            f32(LEVELS, 2, 2 * R, R), f32(3, 2, 2 * R, R), f32(2, 2, R, R), f32(2, 4, R, R), f32(2, 2, R, R),
            f32(4, 2 * R, R), f32(4, 2 * R, R), f32(4, 2 * R, R), f32(4, R, R), f32(8 * R, width), f32(R, width),
            dma((2, 6)), dma((2, 6)), dma((2, 4)), dma((2, 4)), dma((LEVELS,)), dma((LEVELS,)), dma((3,)), dma((3,)),
            dma((4,)), dma((12,)), dma((3,)), dma,
        ],
        compiler_params=pltpu.CompilerParams(
            collective_id=0, has_side_effects=True, vmem_limit_bytes=66_300_000
        ),
        name="tree",
    )(slots, tiles, sketch, wrow, subsketch, couplings)


def per_device(tiles, tile_slots, sketch, row_sketch, subsketch, couplings):
    leaf_basis, transfer, top = run_tree(
        tile_slots.reshape(1, -1), tiles, sketch, row_sketch, subsketch, couplings[0]
    )
    return leaf_basis, transfer[None], top[None]


def solution(mesh):
    return jax.shard_map(
        per_device,
        mesh=mesh,
        in_specs=(
            P(("row", "col"), None, None),
            P(("row", "col")),
            P("col", None),
            P(("row", "col"), None),
            P(),
            P(("row", "col"), None, None, None),
        ),
        out_specs=(
            P(("row", "col"), None),
            P(("row", "col"), None, None, None),
            P(("row", "col"), None, None),
        ),
        check_vma=False,
    )
```

```python
import functools

import jax
import jax.numpy as jnp
from jax import lax
from jax.experimental import pallas as pl
from jax.experimental.pallas import tpu as pltpu
from jax.sharding import PartitionSpec as P

LEVELS = 5
R = 128
F32 = jnp.float32
BF = jnp.bfloat16
HI = lax.Precision.HIGHEST
MESH = pl.DeviceIdType.MESH
LOW, HIGH = pl.ds(0, R), pl.ds(R, R)


def dot(a, b, ca=1, cb=0):
    return lax.dot_general(a, b, (((ca,), (cb,)), ((), ())), precision=HI, preferred_element_type=F32)


def dot16(a, b, ca=1, cb=0):
    return lax.dot_general(a, b, (((ca,), (cb,)), ((), ())), preferred_element_type=F32)


def split3(x):
    hi = x.astype(BF)
    rest = x - hi.astype(F32)
    mid = rest.astype(BF)
    return hi, mid, (rest - mid.astype(F32)).astype(BF)


def dot_bx(b, x, ca=1, cb=0):
    hi, mid, low = split3(x)
    return dot16(b, hi, ca, cb) + (dot16(b, mid, ca, cb) + dot16(b, low, ca, cb))


def dot_xb(x, b, ca=1, cb=0):
    hi, mid, low = split3(x)
    return dot16(hi, b, ca, cb) + (dot16(mid, b, ca, cb) + dot16(low, b, ca, cb))


def row_of(x, k):
    return jnp.broadcast_to(x[k : k + 1, :], x.shape)


def lane_of(x, k):
    return jnp.broadcast_to(x[:, k : k + 1], x.shape)


def factor(t_ref, x_ref, one, segment):
    n = t_ref.shape[0]
    sub = lax.broadcasted_iota(jnp.int32, (8, 128), 0)
    lane = lax.broadcasted_iota(jnp.int32, (8, 128), 1)
    following = t_ref[0]
    cols = [lane_of(following, k) * one for k in range(8)]
    for j in range(n):
        segment(j)
        base = 8 * j
        block = jnp.where(lane == sub + base, 1.0, jnp.where((lane >= base) & (lane < base + 8), 0.0, following))
        rows = [row_of(block, k) for k in range(8)]
        d = [[row_of(cols[k], i) if i >= k else None for k in range(8)] for i in range(8)]
        last = j == n - 1
        if not last:
            nxt = t_ref[j + 1]
            c = [lane_of(nxt, base + k) * one for k in range(8)]
            following = jnp.where((lane >= base) & (lane < base + 8), 0.0, nxt)
            ncols = [lane_of(nxt, base + 8 + k) for k in range(8)]
        inv = []
        mult = [[None] * 8 for _ in range(8)]
        for k in range(8):
            iv = 1.0 / d[k][k]
            inv.append(iv)
            for i in range(k + 1, 8):
                m = d[i][k] * iv
                mult[i][k] = m
                for i2 in range(i, 8):
                    d[i2][i] = d[i2][i] - d[i2][k] * m
                rows[i] = rows[i] - m * rows[k]
                if not last:
                    c[i] = c[i] - m * c[k]
            if not last:
                e = c[k] * iv
                for k2 in range(8):
                    ncols[k2] = ncols[k2] - e * row_of(c[k], k2)
                following = following - e * rows[k]
        out, pivots = rows[0], d[0][0]
        for k in range(1, 8):
            out = jnp.where(sub == k, rows[k], out)
            pivots = jnp.where(sub == k, d[k][k], pivots)
        x_ref[pl.ds(base, 8), :] = jnp.where(lane < base + 8, out * lax.rsqrt(pivots), 0.0)
        if last:
            break
        cols = ncols
        if j < n - 2:
            q = [rows[k] * inv[k] for k in range(8)]
            for k in range(7, 0, -1):
                for i in range(k):
                    q[i] = q[i] - mult[k][i] * q[k]
            for g in range(j + 2, n):
                rest = t_ref[g]
                terms = [lane_of(rest, base + k) * q[k] for k in range(8)]
                while len(terms) > 1:
                    terms = [terms[i] + terms[i + 1] for i in range(0, len(terms), 2)]
                t_ref[g] = jnp.where((lane >= base) & (lane < base + 8), 0.0, rest) - terms[0]


def tree_kernel(
    slots_hbm, tiles_hbm, sketch_hbm, wrow_hbm, subsk_hbm, coup_hbm,
    leaf_out, trans_out, top_out,
    slots, tiles, sketch, wrow, subsk, coup, slot_pad, index_row, index,
    work, linv, gm, zw, ub, comm, comm2, relay, fin, staged, zparts, sparts, vbuf, topbuf, ybuf, ps,
    rs_send, rs_recv, ag_send, ag_recv, c_send, c_recv, c2_send, c2_recv, t_sem, k_sem, i_sem, n_sem,
):
    tile_count = tiles_hbm.shape[0]
    col_tiles = sketch_hbm.shape[0] // R

    def load(src, dst, sem):
        copy = pltpu.make_async_copy(src, dst, sem)
        copy.start()
        return copy

    small = [
        load(src, dst, i_sem.at[i])
        for i, (src, dst) in enumerate([(slots_hbm, slots), (wrow_hbm, wrow), (subsk_hbm, subsk)])
    ]
    per = tile_count // t_sem.shape[0]
    tile_copies = [
        load(tiles_hbm.at[pl.ds(i * per, per)], tiles.at[pl.ds(i * per, per)], t_sem.at[i])
        for i in range(t_sem.shape[0])
    ]
    chunk = sketch_hbm.shape[0] // k_sem.shape[0]

    def load_sketch(first, last):
        for i in range(first, last):
            load(sketch_hbm.at[pl.ds(i * chunk, chunk)], sketch.at[pl.ds(i * chunk, chunk)], k_sem.at[i])

    load_sketch(0, 2)

    slot_pad[...] = jnp.full_like(slot_pad, -1)
    small[0].wait()
    slot_pad[pl.ds(0, 1), pl.ds(0, tile_count)] = slots[...]
    by_tile = jnp.broadcast_to(slot_pad[pl.ds(0, 1), :], (R, slot_pad.shape[1])).T
    which = jnp.minimum(lax.broadcasted_iota(jnp.int32, by_tile.shape, 0), tile_count)
    lane = lax.broadcasted_iota(jnp.int32, by_tile.shape, 1)
    for i in range(index_row.shape[1] // R):
        found = jnp.where(by_tile == lane + i * R, which, tile_count)
        index_row[:, pl.ds(i * R, R)] = jnp.min(found, axis=0, keepdims=True)
    index_copy = load(index_row, index, n_sem)
    tiles[tile_count] = jnp.zeros((R, R), BF)

    row, col = lax.axis_index("row"), lax.axis_index("col")
    position = row * 4 + col
    right, left = (col + 1) % 4, (col + 3) % 4
    across = (col + 2) % 4
    to_right, to_left = (row, right), (row, left)
    chip = row // 2
    core = row - chip * 2
    plane = chip // 4
    x = chip - plane * 4
    x_near = x + 1 - 2 * (x % 2)
    partners = [
        (row, col + 1 - 2 * (col % 2)),
        (row, 3 - col),
        (row + 1 - 2 * core, col),
        ((plane * 4 + x_near) * 2 + core, col),
        ((plane * 4 + 3 - x) * 2 + core, col),
    ]
    upper = [(position // 2**t) % 2 for t in range(LEVELS)]

    barrier = pltpu.get_barrier_semaphore()
    peers = [to_right, to_left] + partners[2:]
    for peer in peers:
        pl.semaphore_signal(barrier, inc=1, device_id=peer, device_id_type=MESH)
    pl.semaphore_wait(barrier, len(peers))

    def remote(src, dst, send, recv, peer):
        return pltpu.make_async_remote_copy(
            src_ref=src, dst_ref=dst, send_sem=send, recv_sem=recv, device_id=peer, device_id_type=MESH
        )

    def rs_copy(parts, n, i):
        src, dst, peer = [
            (parts.at[across, LOW], relay.at[n, 0], to_right),
            (parts.at[across, HIGH], relay.at[n, 1], to_left),
            (parts.at[right, HIGH], fin.at[n, 1], to_right),
            (parts.at[left, LOW], fin.at[n, 2], to_left),
            (staged.at[n, 0], fin.at[n, 0], to_right),
            (staged.at[n, 1], fin.at[n, 3], to_left),
        ][i]
        return remote(src, dst, rs_send.at[n, i], rs_recv.at[n, i], peer)

    def rs_first(parts, n):
        for i in range(4):
            rs_copy(parts, n, i).start()

    def rs_second(parts, n):
        rs_copy(parts, n, 0).wait_recv()
        staged[n, 0] = parts[right, LOW] + relay[n, 0]
        rs_copy(parts, n, 4).start()
        rs_copy(parts, n, 1).wait_recv()
        staged[n, 1] = parts[left, HIGH] + relay[n, 1]
        rs_copy(parts, n, 5).start()

    def rs_last(parts, n, out):
        for i in range(2, 6):
            rs_copy(parts, n, i).wait_recv()
        out[LOW, :] = parts[col, LOW] + (fin[n, 0] + fin[n, 2])
        out[HIGH, :] = parts[col, HIGH] + (fin[n, 1] + fin[n, 3])

    def rs_drain(parts, n):
        for i in range(6):
            rs_copy(parts, n, i).wait_send()

    def ag_copy(buf, n, i, receive=False):
        half = buf.shape[1] // 2
        first, second = pl.ds(0, half), pl.ds(half, half)
        if receive:
            ref = [buf.at[left], buf.at[right], buf.at[across, first], buf.at[across, second]][i]
        else:
            ref = [buf.at[col], buf.at[col], buf.at[left, first], buf.at[right, second]][i]
        return remote(ref, ref, ag_send.at[n, i], ag_recv.at[n, i], [to_right, to_left][i % 2])

    def ag_first(buf, n):
        for i in range(2):
            ag_copy(buf, n, i).start()

    def ag_second(buf, n):
        for i in range(2):
            ag_copy(buf, n, i, True).wait_recv()
            ag_copy(buf, n, i + 2).start()

    def ag_last(buf, n):
        for i in range(2, 4):
            ag_copy(buf, n, i, True).wait_recv()

    def ag_drain(buf, n):
        for i in range(4):
            ag_copy(buf, n, i).wait_send()

    def pair_copy(buf, base, t, send, recv):
        ref = buf.at[t - base, upper[t]]
        return remote(ref, ref, send.at[t - base], recv.at[t - base], partners[t])

    def pair_wait(buf, base, t, send, recv):
        ref = buf.at[t - base, 1 - upper[t]]
        remote(ref, ref, send.at[t - base], recv.at[t - base], partners[t]).wait_recv()

    def leaf_rows(leaf):
        return pl.ds(pl.multiple_of(leaf * 2 * R, R), 2 * R)

    def block_rows(leaf, first, count):
        return jnp.concatenate(
            [
                jnp.concatenate([tiles[index[0, (2 * leaf + i) * col_tiles + first + k]] for k in range(count)], axis=1)
                for i in range(2)
            ],
            axis=0,
        )

    def partial_samples(leaves, count, arriving):
        for leaf in leaves:
            ybuf[leaf_rows(leaf), :] = jnp.zeros((2 * R, ybuf.shape[1]), F32)

        @pl.loop(0, col_tiles // count)
        def _(p):
            rows = pl.ds(pl.multiple_of(p * count * R, R), count * R)
            if arriving:
                pltpu.make_async_copy(sketch_hbm.at[rows], sketch.at[rows], k_sem.at[p]).wait()
            lhs = jnp.concatenate([block_rows(leaf, p * count, count) for leaf in leaves], axis=0)
            product = dot16(lhs, sketch[rows, :])
            for i, leaf in enumerate(leaves):
                ybuf[leaf_rows(leaf), :] += product[i * 2 * R : (i + 1) * 2 * R]

        for leaf in leaves:
            zparts[leaf] = dot(ybuf[leaf_rows(leaf), :], subsk[...])

    small[1].wait()
    small[2].wait()
    zw[:, HIGH] = dot_bx(wrow[...], subsk[...])
    index_copy.wait()
    for copy in tile_copies:
        copy.wait()
    load_sketch(2, k_sem.shape[0])
    small.append(load(coup_hbm, coup, i_sem.at[3]))
    partial_samples([across, right], col_tiles // k_sem.shape[0], True)
    for i in range(3):
        rs_copy(zparts, 0, i).start()
    partial_samples([left], 16, False)
    rs_copy(zparts, 0, 3).start()
    rs_second(zparts, 0)
    partial_samples([col], 16, False)
    small[3].wait()
    rs_last(zparts, 0, zw.at[:, LOW])

    def compose():
        def facing(t, other):
            b = coup[t]
            low = dot_bx(b, other)
            high = dot_bx(b, other, 0, 0)
            return jnp.where(upper[t] == 1, high, low)

        def halves(t):
            own = pl.ds(pl.multiple_of(upper[t] * R, R), R)
            other = pl.ds(pl.multiple_of((1 - upper[t]) * R, R), R)
            return ub[t + 1, own, :], ub[t + 1, other, :]

        own1, other1 = halves(0)
        own2, other2 = halves(1)
        v2 = dot(own1, own2)
        c2 = -(dot(facing(0, other1), own2) + dot(own1, facing(1, other2)))
        base = ub[0]
        v = dot(base, v2)
        vbuf[col] = v
        ag_first(vbuf, 0)
        c = dot(base, c2)
        w = wrow[...]
        ps[...] = dot_xb(c, w, 0, 0)
        pp = dot_xb(v, w, 0, 0)
        for k in range(4):
            sparts[k, HIGH] = pp[:, k * R : (k + 1) * R]

    def relay_bases():
        ag_second(vbuf, 0)

    def wide_parts():
        ag_last(vbuf, 0)

        @pl.loop(0, 4)
        def _(k):
            rows = pl.ds(pl.multiple_of(k * 2 * R, R), 2 * R)
            ps[...] += dot(vbuf[k], ybuf[rows, :], 0, 0)

        for k in range(4):
            sparts[k, LOW] = ps[:, k * R : (k + 1) * R]
        rs_first(sparts, 1)

    def relay_parts():
        rs_second(sparts, 1)

    def wide_start():
        rs_last(sparts, 1, comm2.at[0, upper[2]])
        pair_copy(comm2, 2, 2, c2_send, c2_recv).start()

    def wide_merge(t):
        pair_wait(comm2, 2, t, c2_send, c2_recv)
        low_p, high_p = comm2[t - 2, 0, HIGH], comm2[t - 2, 1, HIGH]
        low = comm2[t - 2, 0, LOW] - dot_bx(coup[t], high_p)
        high = comm2[t - 2, 1, LOW] - dot_bx(coup[t], low_p, 0, 0)
        u_low, u_high = ub[t + 1, LOW, :], ub[t + 1, HIGH, :]
        sample = dot(u_low, low, 0, 0) + dot(u_high, high, 0, 0)
        if t == LEVELS - 1:
            topbuf[col] = sample
            return
        comm2[t - 1, upper[t + 1], LOW] = sample
        comm2[t - 1, upper[t + 1], HIGH] = dot(u_low, low_p, 0, 0) + dot(u_high, high_p, 0, 0)
        pair_copy(comm2, 2, t + 1, c2_send, c2_recv).start()

    at_start = {4: relay_parts, 5: functools.partial(wide_merge, 3)}
    at_middle = {3: relay_bases, 4: wide_start}
    at_end = {2: compose, 3: wide_parts, 4: functools.partial(wide_merge, 2)}

    def place(table, t):
        for at, piece in table.items():
            pl.when(t == at)(piece)

    i0 = lax.broadcasted_iota(jnp.int32, (16, 8, R), 0) * 8 + lax.broadcasted_iota(jnp.int32, (16, 8, R), 1)
    eye = i0 == lax.broadcasted_iota(jnp.int32, (16, 8, R), 2)
    one = jnp.broadcast_to(jnp.where(position >= 0, 1.0, 0.0).astype(F32), (8, R))
    pieces = 4
    piece = R // pieces

    def of_level(t, values):
        return sum(jnp.where(t == k, value, 0) for k, value in enumerate(values))

    def stage(t, carry):
        own = of_level(t, upper)
        peer = (of_level(t, [p[0] for p in partners]), of_level(t, [p[1] for p in partners]))
        below = t - 1

        def piece_copy(level, side, i):
            ref = comm.at[level, side, pl.ds(i * piece, piece), :]
            return remote(ref, ref, c_send.at[level, i], c_recv.at[level, i], peer)

        @pl.when(t > 0)
        def _():
            own_below = of_level(below, upper)
            for i in range(pieces):
                piece_copy(below, 1 - own_below, i).wait_recv()
            b = coup[below]
            low_w, high_w = comm[below, 0, :, HIGH], comm[below, 1, :, HIGH]
            zw[LOW, LOW] = comm[below, 0, :, LOW] - dot_bx(b, high_w)
            zw[HIGH, LOW] = comm[below, 1, :, LOW] - dot_bx(b, low_w, 0, 0)
            zw[LOW, HIGH] = low_w
            zw[HIGH, HIGH] = high_w

        place(at_start, t)
        z = zw[:, LOW]
        products = dot(z, zw[...], 0, 0)
        gm[...] = products
        shift = 0.0001 * jnp.sum(z * z, keepdims=True) / R + 1e-06
        work[...] = products[:, :R].reshape(16, 8, R) + jnp.where(eye, shift.reshape(1, 1, 1), 0.0)

        def make_piece(i):
            rows = pl.ds(i * piece, piece)
            comm[t, own, rows, :] = dot(linv[rows, :], gm[...])

        def send_piece(i):
            @pl.when(t < LEVELS)
            def _():
                piece_copy(t, own, i).start()

        def segment(j):
            if j == 8:
                place(at_middle, t)
            if j % 4 == 2 and j > 4:
                send_piece(j // 4 - 1)
            if j % 4 == 0 and j > 0:
                make_piece(j // 4 - 1)

        factor(work, linv, one, segment)
        make_piece(pieces - 1)
        send_piece(pieces - 1)
        u = dot(zw[:, LOW], linv[...], 1, 1)
        ub[t] = u

        @pl.when(t == 0)
        def _():
            leaf_out[...] = u

        @pl.when(t > 0)
        def _():
            half = pl.ds(pl.multiple_of(of_level(below, upper) * R, R), R)
            trans_out[below] = ub[t, half, :]

        place(at_end, t)
        return carry

    lax.fori_loop(0, LEVELS + 1, stage, 0)
    wide_merge(LEVELS - 1)
    ag_first(topbuf, 1)
    ag_second(topbuf, 1)
    ag_last(topbuf, 1)
    for k in range(4):
        top_out[:, pl.ds(k * R, R)] = topbuf[k]

    rs_drain(zparts, 0)
    rs_drain(sparts, 1)
    ag_drain(vbuf, 0)
    ag_drain(topbuf, 1)
    for t in range(LEVELS):
        for i in range(pieces):
            ref = comm.at[t, upper[t], pl.ds(i * piece, piece), :]
            remote(ref, ref, c_send.at[t, i], c_recv.at[t, i], partners[t]).wait_send()
    for t in range(2, LEVELS):
        pair_copy(comm2, 2, t, c2_send, c2_recv).wait_send()


def run_tree(slots, tiles, sketch, wrow, subsketch, couplings):
    vmem = pl.BlockSpec(memory_space=pltpu.VMEM)
    hbm = pl.BlockSpec(memory_space=pltpu.HBM)
    dma = pltpu.SemaphoreType.DMA
    tile_count = tiles.shape[0]
    depth, width = sketch.shape
    slot_count = 8 * depth // R

    def f32(*shape):
        return pltpu.VMEM(shape, F32)

    return pl.pallas_call(
        tree_kernel,
        out_shape=[
            jax.ShapeDtypeStruct((2 * R, R), F32),
            jax.ShapeDtypeStruct((LEVELS, R, R), F32),
            jax.ShapeDtypeStruct((R, width), F32),
        ],
        in_specs=[hbm] * 6,
        out_specs=[vmem, vmem, vmem],
        scratch_shapes=[
            pltpu.VMEM(slots.shape, jnp.int32), pltpu.VMEM((tile_count + 1, R, R), BF), pltpu.VMEM((depth, width), BF), pltpu.VMEM(wrow.shape, BF),
            f32(width, R), pltpu.VMEM(couplings.shape, BF), pltpu.VMEM((1, 2 * R), jnp.int32),
            pltpu.VMEM((1, slot_count), jnp.int32), pltpu.SMEM((1, slot_count), jnp.int32),
            f32(16, 8, R), f32(R, R), f32(R, 2 * R), f32(2 * R, 2 * R), f32(LEVELS + 1, 2 * R, R),
            f32(LEVELS + 1, 2, R, 2 * R), f32(3, 2, 2 * R, R), f32(2, 2, R, R), f32(2, 4, R, R), f32(2, 2, R, R),
            f32(4, 2 * R, R), f32(4, 2 * R, R), f32(4, 2 * R, R), f32(4, R, R), f32(8 * R, width), f32(R, width),
            dma((2, 6)), dma((2, 6)), dma((2, 4)), dma((2, 4)), dma((LEVELS, 4)), dma((LEVELS, 4)), dma((3,)), dma((3,)),
            dma((4,)), dma((6,)), dma((4,)), dma,
        ],
        compiler_params=pltpu.CompilerParams(
            collective_id=0, has_side_effects=True, vmem_limit_bytes=48 * 2**20
        ),
        name="tree",
    )(*[pltpu.with_memory_space_constraint(a, pltpu.HBM) for a in (slots, tiles, sketch, wrow, subsketch, couplings)])


def per_device(tiles, tile_slots, sketch, row_sketch, subsketch, couplings):
    leaf_basis, transfer, top = run_tree(
        tile_slots.reshape(1, -1), tiles, sketch, row_sketch, subsketch, couplings[0]
    )
    return leaf_basis, transfer[None], top[None]


def solution(mesh):
    return jax.shard_map(
        per_device,
        mesh=mesh,
        in_specs=(
            P(("row", "col"), None, None),
            P(("row", "col")),
            P("col", None),
            P(("row", "col"), None),
            P(),
            P(("row", "col"), None, None, None),
        ),
        out_specs=(
            P(("row", "col"), None),
            P(("row", "col"), None, None, None),
            P(("row", "col"), None, None),
        ),
        check_vma=False,
    )
```

```python
import functools

import jax
import jax.numpy as jnp
from jax import lax
from jax.experimental import pallas as pl
from jax.experimental.pallas import tpu as pltpu
from jax.sharding import PartitionSpec as P

LEVELS = 5
R = 128
F32 = jnp.float32
BF = jnp.bfloat16
HI = lax.Precision.HIGHEST
MESH = pl.DeviceIdType.MESH
LOW, HIGH = pl.ds(0, R), pl.ds(R, R)


def dot(a, b, ca=1, cb=0):
    return lax.dot_general(a, b, (((ca,), (cb,)), ((), ())), precision=HI, preferred_element_type=F32)


def dot16(a, b, ca=1, cb=0):
    return lax.dot_general(a, b, (((ca,), (cb,)), ((), ())), preferred_element_type=F32)


def split3(x):
    hi = x.astype(BF)
    rest = x - hi.astype(F32)
    mid = rest.astype(BF)
    return hi, mid, (rest - mid.astype(F32)).astype(BF)


def dot_bx(b, x, ca=1, cb=0):
    hi, mid, low = split3(x)
    return dot16(b, hi, ca, cb) + (dot16(b, mid, ca, cb) + dot16(b, low, ca, cb))


def dot_xb(x, b, ca=1, cb=0):
    hi, mid, low = split3(x)
    return dot16(hi, b, ca, cb) + (dot16(mid, b, ca, cb) + dot16(low, b, ca, cb))


def row_of(x, k):
    return jnp.broadcast_to(x[k : k + 1, :], x.shape)


def lane_of(x, k):
    return jnp.broadcast_to(x[:, k : k + 1], x.shape)


def factor(t_ref, x_ref, one, segment):
    n = t_ref.shape[0]
    sub = lax.broadcasted_iota(jnp.int32, (8, 128), 0)
    lane = lax.broadcasted_iota(jnp.int32, (8, 128), 1)
    following = t_ref[0]
    cols = [lane_of(following, k) * one for k in range(8)]
    for j in range(n):
        segment(j)
        base = 8 * j
        block = jnp.where(lane == sub + base, 1.0, jnp.where((lane >= base) & (lane < base + 8), 0.0, following))
        rows = [row_of(block, k) for k in range(8)]
        d = [[row_of(cols[k], i) if i >= k else None for k in range(8)] for i in range(8)]
        last = j == n - 1
        if not last:
            nxt = t_ref[j + 1]
            c = [lane_of(nxt, base + k) * one for k in range(8)]
            following = jnp.where((lane >= base) & (lane < base + 8), 0.0, nxt)
            ncols = [lane_of(nxt, base + 8 + k) for k in range(8)]
        inv = []
        mult = [[None] * 8 for _ in range(8)]
        for k in range(8):
            iv = 1.0 / d[k][k]
            inv.append(iv)
            for i in range(k + 1, 8):
                m = d[i][k] * iv
                mult[i][k] = m
                for i2 in range(i, 8):
                    d[i2][i] = d[i2][i] - d[i2][k] * m
                rows[i] = rows[i] - m * rows[k]
                if not last:
                    c[i] = c[i] - m * c[k]
            if not last:
                e = c[k] * iv
                for k2 in range(8):
                    ncols[k2] = ncols[k2] - e * row_of(c[k], k2)
                following = following - e * rows[k]
        out, pivots = rows[0], d[0][0]
        for k in range(1, 8):
            out = jnp.where(sub == k, rows[k], out)
            pivots = jnp.where(sub == k, d[k][k], pivots)
        x_ref[pl.ds(base, 8), :] = jnp.where(lane < base + 8, out * lax.rsqrt(pivots), 0.0)
        if last:
            break
        cols = ncols
        if j < n - 2:
            q = [rows[k] * inv[k] for k in range(8)]
            for k in range(7, 0, -1):
                for i in range(k):
                    q[i] = q[i] - mult[k][i] * q[k]
            for g in range(j + 2, n):
                rest = t_ref[g]
                terms = [lane_of(rest, base + k) * q[k] for k in range(8)]
                while len(terms) > 1:
                    terms = [terms[i] + terms[i + 1] for i in range(0, len(terms), 2)]
                t_ref[g] = jnp.where((lane >= base) & (lane < base + 8), 0.0, rest) - terms[0]


def tree_kernel(
    slots_hbm, tiles_hbm, sketch_hbm, wrow_hbm, subsk_hbm, coup_hbm,
    leaf_out, trans_out, top_out,
    slots, tiles, sketch, wrow, subsk, coup, slot_pad, index_row, index,
    work, linv, gm, zw, ub, comm, comm2, relay, fin, staged, zparts, sparts, vbuf, topbuf, ybuf, p0, s0, u1, down,
    rs_send, rs_recv, ag_send, ag_recv, c_send, c_recv, c2_send, c2_recv, u_send, u_recv, t_sem, k_sem, i_sem, n_sem,
):
    tile_count = tiles_hbm.shape[0]
    col_tiles = sketch_hbm.shape[0] // R

    def load(src, dst, sem):
        copy = pltpu.make_async_copy(src, dst, sem)
        copy.start()
        return copy

    small = [
        load(src, dst, i_sem.at[i])
        for i, (src, dst) in enumerate([(slots_hbm, slots), (wrow_hbm, wrow), (subsk_hbm, subsk)])
    ]
    per = tile_count // t_sem.shape[0]
    tile_copies = [
        load(tiles_hbm.at[pl.ds(i * per, per)], tiles.at[pl.ds(i * per, per)], t_sem.at[i])
        for i in range(t_sem.shape[0])
    ]
    chunk = sketch_hbm.shape[0] // k_sem.shape[0]

    def load_sketch(first, last):
        for i in range(first, last):
            load(sketch_hbm.at[pl.ds(i * chunk, chunk)], sketch.at[pl.ds(i * chunk, chunk)], k_sem.at[i])

    load_sketch(0, 2)

    slot_pad[...] = jnp.full_like(slot_pad, -1)
    small[0].wait()
    slot_pad[pl.ds(0, 1), pl.ds(0, tile_count)] = slots[...]
    by_tile = jnp.broadcast_to(slot_pad[pl.ds(0, 1), :], (R, slot_pad.shape[1])).T
    which = jnp.minimum(lax.broadcasted_iota(jnp.int32, by_tile.shape, 0), tile_count)
    lane = lax.broadcasted_iota(jnp.int32, by_tile.shape, 1)
    for i in range(index_row.shape[1] // R):
        found = jnp.where(by_tile == lane + i * R, which, tile_count)
        index_row[:, pl.ds(i * R, R)] = jnp.min(found, axis=0, keepdims=True)
    index_copy = load(index_row, index, n_sem)
    tiles[tile_count] = jnp.zeros((R, R), BF)

    row, col = lax.axis_index("row"), lax.axis_index("col")
    position = row * 4 + col
    right, left = (col + 1) % 4, (col + 3) % 4
    across = (col + 2) % 4
    to_right, to_left = (row, right), (row, left)
    chip = row // 2
    core = row - chip * 2
    plane = chip // 4
    x = chip - plane * 4
    x_near = x + 1 - 2 * (x % 2)
    partners = [
        (row, col + 1 - 2 * (col % 2)),
        (row, 3 - col),
        (row + 1 - 2 * core, col),
        ((plane * 4 + x_near) * 2 + core, col),
        ((plane * 4 + 3 - x) * 2 + core, col),
    ]
    upper = [(position // 2**t) % 2 for t in range(LEVELS)]

    barrier = pltpu.get_barrier_semaphore()
    peers = [to_right, to_left] + partners[2:]
    for peer in peers:
        pl.semaphore_signal(barrier, inc=1, device_id=peer, device_id_type=MESH)
    pl.semaphore_wait(barrier, len(peers))

    def remote(src, dst, send, recv, peer):
        return pltpu.make_async_remote_copy(
            src_ref=src, dst_ref=dst, send_sem=send, recv_sem=recv, device_id=peer, device_id_type=MESH
        )

    def rs_copy(parts, n, i):
        src, dst, peer = [
            (parts.at[across, LOW], relay.at[n, 0], to_right),
            (parts.at[across, HIGH], relay.at[n, 1], to_left),
            (parts.at[right, HIGH], fin.at[n, 1], to_right),
            (parts.at[left, LOW], fin.at[n, 2], to_left),
            (staged.at[n, 0], fin.at[n, 0], to_right),
            (staged.at[n, 1], fin.at[n, 3], to_left),
        ][i]
        return remote(src, dst, rs_send.at[n, i], rs_recv.at[n, i], peer)

    def rs_first(parts, n):
        for i in range(4):
            rs_copy(parts, n, i).start()

    def rs_second(parts, n):
        rs_copy(parts, n, 0).wait_recv()
        staged[n, 0] = parts[right, LOW] + relay[n, 0]
        rs_copy(parts, n, 4).start()
        rs_copy(parts, n, 1).wait_recv()
        staged[n, 1] = parts[left, HIGH] + relay[n, 1]
        rs_copy(parts, n, 5).start()

    def rs_last(parts, n, out):
        for i in range(2, 6):
            rs_copy(parts, n, i).wait_recv()
        out[LOW, :] = parts[col, LOW] + (fin[n, 0] + fin[n, 2])
        out[HIGH, :] = parts[col, HIGH] + (fin[n, 1] + fin[n, 3])

    def rs_drain(parts, n):
        for i in range(6):
            rs_copy(parts, n, i).wait_send()

    def ag_copy(buf, n, i, receive=False):
        half = buf.shape[1] // 2
        first, second = pl.ds(0, half), pl.ds(half, half)
        if receive:
            ref = [buf.at[left], buf.at[right], buf.at[across, first], buf.at[across, second]][i]
        else:
            ref = [buf.at[col], buf.at[col], buf.at[left, first], buf.at[right, second]][i]
        return remote(ref, ref, ag_send.at[n, i], ag_recv.at[n, i], [to_right, to_left][i % 2])

    def ag_first(buf, n):
        for i in range(2):
            ag_copy(buf, n, i).start()

    def ag_second(buf, n):
        for i in range(2):
            ag_copy(buf, n, i, True).wait_recv()
            ag_copy(buf, n, i + 2).start()

    def ag_last(buf, n):
        for i in range(2, 4):
            ag_copy(buf, n, i, True).wait_recv()

    def ag_drain(buf, n):
        for i in range(4):
            ag_copy(buf, n, i).wait_send()

    def pair_copy(buf, base, t, send, recv):
        ref = buf.at[t - base, upper[t]]
        return remote(ref, ref, send.at[t - base], recv.at[t - base], partners[t])

    def pair_wait(buf, base, t, send, recv):
        ref = buf.at[t - base, 1 - upper[t]]
        remote(ref, ref, send.at[t - base], recv.at[t - base], partners[t]).wait_recv()

    def leaf_rows(leaf):
        return pl.ds(pl.multiple_of(leaf * 2 * R, R), 2 * R)

    def block_rows(leaf, first, count):
        return jnp.concatenate(
            [
                jnp.concatenate([tiles[index[0, (2 * leaf + i) * col_tiles + first + k]] for k in range(count)], axis=1)
                for i in range(2)
            ],
            axis=0,
        )

    def partial_samples(leaves, count, arriving):
        for leaf in leaves:
            ybuf[leaf_rows(leaf), :] = jnp.zeros((2 * R, ybuf.shape[1]), F32)

        @pl.loop(0, col_tiles // count)
        def _(p):
            rows = pl.ds(pl.multiple_of(p * count * R, R), count * R)
            if arriving:
                pltpu.make_async_copy(sketch_hbm.at[rows], sketch.at[rows], k_sem.at[p]).wait()
            lhs = jnp.concatenate([block_rows(leaf, p * count, count) for leaf in leaves], axis=0)
            product = dot16(lhs, sketch[rows, :])
            for i, leaf in enumerate(leaves):
                ybuf[leaf_rows(leaf), :] += product[i * 2 * R : (i + 1) * 2 * R]

        for leaf in leaves:
            zparts[leaf] = dot(ybuf[leaf_rows(leaf), :], subsk[...])

    small[1].wait()
    small[2].wait()
    zw[:, HIGH] = dot_bx(wrow[...], subsk[...])
    index_copy.wait()
    for copy in tile_copies:
        copy.wait()
    load_sketch(2, k_sem.shape[0])
    small.append(load(coup_hbm, coup, i_sem.at[3]))
    partial_samples([across], col_tiles // k_sem.shape[0], True)
    for i in range(2):
        rs_copy(zparts, 0, i).start()
    partial_samples([right, left], 8, False)
    for i in range(2, 4):
        rs_copy(zparts, 0, i).start()
    rs_second(zparts, 0)
    partial_samples([col], 16, False)
    small[3].wait()
    rs_last(zparts, 0, zw.at[:, LOW])

    def share_leaf():
        vbuf[col] = ub[0]
        ag_first(vbuf, 0)
        p0[...] = dot_xb(ub[0], wrow[...], 0, 0)

    def leaf_part(leaf):
        rows = pl.ds(pl.multiple_of(leaf * R, R), R)
        s0[rows, :] = dot(vbuf[leaf], ybuf[leaf_rows(leaf), :], 0, 0)

    def pair_bases():
        ref = u1.at[upper[1]]
        return remote(ref, ref, u_send, u_recv, partners[1])

    def share_pair():
        u1[upper[1]] = ub[1]
        pair_bases().start()
        ag_second(vbuf, 0)
        leaf_part(col)
        leaf_part(left)
        leaf_part(right)

    def wide_parts():
        def facing(t, other):
            b = coup[t]
            return jnp.where(upper[t] == 1, dot_bx(b, other, 0, 0), dot_bx(b, other))

        def halves(t):
            own = pl.ds(pl.multiple_of(upper[t] * R, R), R)
            other = pl.ds(pl.multiple_of((1 - upper[t]) * R, R), R)
            return ub[t + 1, own, :], ub[t + 1, other, :]

        ag_last(vbuf, 0)
        leaf_part(across)
        own1, other1 = halves(0)
        own2, other2 = halves(1)
        correction = -(dot(facing(0, other1), own2) + dot(own1, facing(1, other2)))
        ref = u1.at[1 - upper[1]]
        remote(ref, ref, u_send, u_recv, partners[1]).wait_recv()
        down[pl.ds(0, 2 * R), :] = dot(u1[0], ub[2, LOW, :])
        down[pl.ds(2 * R, 2 * R), :] = dot(u1[1], ub[2, HIGH, :])
        sample = dot(down[...], s0[...], 0, 0) + dot(correction, p0[...], 0, 0)
        proj = dot(down[pl.ds(pl.multiple_of(col * R, R), R), :], p0[...], 0, 0)
        for k in range(4):
            sparts[k, LOW] = sample[:, k * R : (k + 1) * R]
            sparts[k, HIGH] = proj[:, k * R : (k + 1) * R]
        rs_first(sparts, 1)

    def relay_parts():
        rs_second(sparts, 1)

    def wide_start():
        rs_last(sparts, 1, comm2.at[0, upper[2]])
        pair_copy(comm2, 2, 2, c2_send, c2_recv).start()
        wide_merge(2)

    def wide_merge(t):
        pair_wait(comm2, 2, t, c2_send, c2_recv)
        low_p, high_p = comm2[t - 2, 0, HIGH], comm2[t - 2, 1, HIGH]
        low = comm2[t - 2, 0, LOW] - dot_bx(coup[t], high_p)
        high = comm2[t - 2, 1, LOW] - dot_bx(coup[t], low_p, 0, 0)
        u_low, u_high = ub[t + 1, LOW, :], ub[t + 1, HIGH, :]
        sample = dot(u_low, low, 0, 0) + dot(u_high, high, 0, 0)
        if t == LEVELS - 1:
            topbuf[col] = sample
            return
        comm2[t - 1, upper[t + 1], LOW] = sample
        comm2[t - 1, upper[t + 1], HIGH] = dot(u_low, low_p, 0, 0) + dot(u_high, high_p, 0, 0)
        pair_copy(comm2, 2, t + 1, c2_send, c2_recv).start()

    at_middle = {3: relay_parts}
    at_end = {0: share_leaf, 1: share_pair, 2: wide_parts, 3: wide_start, 4: functools.partial(wide_merge, 3)}

    def place(table, t):
        for at, piece in table.items():
            pl.when(t == at)(piece)

    i0 = lax.broadcasted_iota(jnp.int32, (16, 8, R), 0) * 8 + lax.broadcasted_iota(jnp.int32, (16, 8, R), 1)
    eye = i0 == lax.broadcasted_iota(jnp.int32, (16, 8, R), 2)
    one = jnp.broadcast_to(jnp.where(position >= 0, 1.0, 0.0).astype(F32), (8, R))
    pieces = 4
    piece = R // pieces

    def of_level(t, values):
        return sum(jnp.where(t == k, value, 0) for k, value in enumerate(values))

    def stage(t, carry):
        own = of_level(t, upper)
        peer = (of_level(t, [p[0] for p in partners]), of_level(t, [p[1] for p in partners]))
        below = t - 1

        def piece_copy(level, side, i):
            ref = comm.at[level, side, pl.ds(i * piece, piece), :]
            return remote(ref, ref, c_send.at[level, i], c_recv.at[level, i], peer)

        @pl.when(t > 0)
        def _():
            own_below = of_level(below, upper)
            for i in range(pieces):
                piece_copy(below, 1 - own_below, i).wait_recv()
            b = coup[below]
            low_w, high_w = comm[below, 0, :, HIGH], comm[below, 1, :, HIGH]
            zw[LOW, LOW] = comm[below, 0, :, LOW] - dot_bx(b, high_w)
            zw[HIGH, LOW] = comm[below, 1, :, LOW] - dot_bx(b, low_w, 0, 0)
            zw[LOW, HIGH] = low_w
            zw[HIGH, HIGH] = high_w

        z = zw[:, LOW]
        products = dot(z, zw[...], 0, 0)
        gm[...] = products
        shift = 0.0001 * jnp.sum(z * z, keepdims=True) / R + 1e-06
        work[...] = products[:, :R].reshape(16, 8, R) + jnp.where(eye, shift.reshape(1, 1, 1), 0.0)

        def make_piece(i):
            rows = pl.ds(i * piece, piece)
            comm[t, own, rows, :] = dot(linv[rows, :], gm[...])

        def send_piece(i):
            @pl.when(t < LEVELS)
            def _():
                piece_copy(t, own, i).start()

        def segment(j):
            if j == 8:
                place(at_middle, t)
            if j % 4 == 2 and j > 4:
                send_piece(j // 4 - 1)
            if j % 4 == 0 and j > 0:
                make_piece(j // 4 - 1)

        factor(work, linv, one, segment)
        make_piece(pieces - 1)
        send_piece(pieces - 1)
        u = dot(zw[:, LOW], linv[...], 1, 1)
        ub[t] = u

        @pl.when(t == 0)
        def _():
            leaf_out[...] = u

        @pl.when(t > 0)
        def _():
            half = pl.ds(pl.multiple_of(of_level(below, upper) * R, R), R)
            trans_out[below] = ub[t, half, :]

        place(at_end, t)
        return carry

    lax.fori_loop(0, LEVELS + 1, stage, 0)
    wide_merge(LEVELS - 1)
    ag_first(topbuf, 1)
    ag_second(topbuf, 1)
    ag_last(topbuf, 1)
    for k in range(4):
        top_out[:, pl.ds(k * R, R)] = topbuf[k]

    rs_drain(zparts, 0)
    rs_drain(sparts, 1)
    ag_drain(vbuf, 0)
    pair_bases().wait_send()
    ag_drain(topbuf, 1)
    for t in range(LEVELS):
        for i in range(pieces):
            ref = comm.at[t, upper[t], pl.ds(i * piece, piece), :]
            remote(ref, ref, c_send.at[t, i], c_recv.at[t, i], partners[t]).wait_send()
    for t in range(2, LEVELS):
        pair_copy(comm2, 2, t, c2_send, c2_recv).wait_send()


def run_tree(slots, tiles, sketch, wrow, subsketch, couplings):
    vmem = pl.BlockSpec(memory_space=pltpu.VMEM)
    hbm = pl.BlockSpec(memory_space=pltpu.HBM)
    dma = pltpu.SemaphoreType.DMA
    tile_count = tiles.shape[0]
    depth, width = sketch.shape
    slot_count = 8 * depth // R

    def f32(*shape):
        return pltpu.VMEM(shape, F32)

    return pl.pallas_call(
        tree_kernel,
        out_shape=[
            jax.ShapeDtypeStruct((2 * R, R), F32),
            jax.ShapeDtypeStruct((LEVELS, R, R), F32),
            jax.ShapeDtypeStruct((R, width), F32),
        ],
        in_specs=[hbm] * 6,
        out_specs=[vmem, vmem, vmem],
        scratch_shapes=[
            pltpu.VMEM(slots.shape, jnp.int32), pltpu.VMEM((tile_count + 1, R, R), BF), pltpu.VMEM((depth, width), BF), pltpu.VMEM(wrow.shape, BF),
            f32(width, R), pltpu.VMEM(couplings.shape, BF), pltpu.VMEM((1, 2 * R), jnp.int32),
            pltpu.VMEM((1, slot_count), jnp.int32), pltpu.SMEM((1, slot_count), jnp.int32),
            f32(16, 8, R), f32(R, R), f32(R, 2 * R), f32(2 * R, 2 * R), f32(LEVELS + 1, 2 * R, R),
            f32(LEVELS + 1, 2, R, 2 * R), f32(3, 2, 2 * R, R), f32(2, 2, R, R), f32(2, 4, R, R), f32(2, 2, R, R),
            f32(4, 2 * R, R), f32(4, 2 * R, R), f32(4, 2 * R, R), f32(4, R, R), f32(8 * R, width), f32(R, width),
            f32(4 * R, width), f32(2, 2 * R, R), f32(4 * R, R),
            dma((2, 6)), dma((2, 6)), dma((2, 4)), dma((2, 4)), dma((LEVELS, 4)), dma((LEVELS, 4)), dma((3,)), dma((3,)), dma, dma,
            dma((4,)), dma((6,)), dma((4,)), dma,
        ],
        compiler_params=pltpu.CompilerParams(
            collective_id=0, has_side_effects=True, vmem_limit_bytes=48 * 2**20
        ),
        name="tree",
    )(*[pltpu.with_memory_space_constraint(a, pltpu.HBM) for a in (slots, tiles, sketch, wrow, subsketch, couplings)])


def per_device(tiles, tile_slots, sketch, row_sketch, subsketch, couplings):
    leaf_basis, transfer, top = run_tree(
        tile_slots.reshape(1, -1), tiles, sketch, row_sketch, subsketch, couplings[0]
    )
    return leaf_basis, transfer[None], top[None]


def solution(mesh):
    return jax.shard_map(
        per_device,
        mesh=mesh,
        in_specs=(
            P(("row", "col"), None, None),
            P(("row", "col")),
            P("col", None),
            P(("row", "col"), None),
            P(),
            P(("row", "col"), None, None, None),
        ),
        out_specs=(
            P(("row", "col"), None),
            P(("row", "col"), None, None, None),
            P(("row", "col"), None, None),
        ),
        check_vma=False,
    )
```

```python
import functools

import jax
import jax.numpy as jnp
from jax import lax
from jax.experimental import pallas as pl
from jax.experimental.pallas import tpu as pltpu
from jax.sharding import PartitionSpec as P

LEVELS = 5
R = 128
F32 = jnp.float32
BF = jnp.bfloat16
HI = lax.Precision.HIGHEST
MESH = pl.DeviceIdType.MESH
LOW, HIGH = pl.ds(0, R), pl.ds(R, R)


def dot(a, b, ca=1, cb=0):
    return lax.dot_general(a, b, (((ca,), (cb,)), ((), ())), precision=HI, preferred_element_type=F32)


def dot16(a, b, ca=1, cb=0):
    return lax.dot_general(a, b, (((ca,), (cb,)), ((), ())), preferred_element_type=F32)


def split3(x):
    hi = x.astype(BF)
    rest = x - hi.astype(F32)
    mid = rest.astype(BF)
    return hi, mid, (rest - mid.astype(F32)).astype(BF)


def split2(x):
    hi = x.astype(BF)
    return hi, (x - hi.astype(F32)).astype(BF)


def dot3(a, b, ca=1, cb=0):
    a_hi, a_lo = split2(a)
    b_hi, b_lo = split2(b)
    return dot16(a_hi, b_hi, ca, cb) + (dot16(a_hi, b_lo, ca, cb) + dot16(a_lo, b_hi, ca, cb))


def dot_bx(b, x, ca=1, cb=0):
    hi, mid, low = split3(x)
    return dot16(b, hi, ca, cb) + (dot16(b, mid, ca, cb) + dot16(b, low, ca, cb))


def dot_xb(x, b, ca=1, cb=0):
    hi, mid, low = split3(x)
    return dot16(hi, b, ca, cb) + (dot16(mid, b, ca, cb) + dot16(low, b, ca, cb))


def row_of(x, k):
    return jnp.broadcast_to(x[k : k + 1, :], x.shape)


def lane_of(x, k):
    return jnp.broadcast_to(x[:, k : k + 1], x.shape)


def factor(t_ref, x_ref, one, segment):
    n = t_ref.shape[0]
    sub = lax.broadcasted_iota(jnp.int32, (8, 128), 0)
    lane = lax.broadcasted_iota(jnp.int32, (8, 128), 1)
    following = t_ref[0]
    cols = [lane_of(following, k) * one for k in range(8)]
    for j in range(n):
        segment(j)
        base = 8 * j
        block = jnp.where(lane == sub + base, 1.0, jnp.where((lane >= base) & (lane < base + 8), 0.0, following))
        rows = [row_of(block, k) for k in range(8)]
        d = [[row_of(cols[k], i) if i >= k else None for k in range(8)] for i in range(8)]
        last = j == n - 1
        if not last:
            nxt = t_ref[j + 1]
            c = [lane_of(nxt, base + k) * one for k in range(8)]
            following = jnp.where((lane >= base) & (lane < base + 8), 0.0, nxt)
            ncols = [lane_of(nxt, base + 8 + k) for k in range(8)]
        inv = []
        mult = [[None] * 8 for _ in range(8)]
        for k in range(8):
            iv = 1.0 / d[k][k]
            inv.append(iv)
            for i in range(k + 1, 8):
                m = d[i][k] * iv
                mult[i][k] = m
                for i2 in range(i, 8):
                    d[i2][i] = d[i2][i] - d[i2][k] * m
                rows[i] = rows[i] - m * rows[k]
                if not last:
                    c[i] = c[i] - m * c[k]
            if not last:
                e = c[k] * iv
                for k2 in range(8):
                    ncols[k2] = ncols[k2] - e * row_of(c[k], k2)
                following = following - e * rows[k]
        out, pivots = rows[0], d[0][0]
        for k in range(1, 8):
            out = jnp.where(sub == k, rows[k], out)
            pivots = jnp.where(sub == k, d[k][k], pivots)
        x_ref[pl.ds(base, 8), :] = jnp.where(lane < base + 8, out * lax.rsqrt(pivots), 0.0)
        if last:
            break
        cols = ncols
        if j < n - 2:
            q = [rows[k] * inv[k] for k in range(8)]
            for k in range(7, 0, -1):
                for i in range(k):
                    q[i] = q[i] - mult[k][i] * q[k]
            for g in range(j + 2, n):
                rest = t_ref[g]
                terms = [lane_of(rest, base + k) * q[k] for k in range(8)]
                while len(terms) > 1:
                    terms = [terms[i] + terms[i + 1] for i in range(0, len(terms), 2)]
                t_ref[g] = jnp.where((lane >= base) & (lane < base + 8), 0.0, rest) - terms[0]


def tree_kernel(
    slots_hbm, tiles_hbm, sketch_hbm, wrow_hbm, subsk_hbm, coup_hbm,
    leaf_out, trans_out, top_out,
    slots, tiles, sketch, wrow, subsk, coup, slot_pad, index_row, index,
    work, linv, gm, zw, ub, comm, comm2, relay, fin, staged, zparts, sparts, vbuf, topbuf, ybuf, p0, s0, u1, down, pq,
    rs_send, rs_recv, ag_send, ag_recv, c_send, c_recv, c2_send, c2_recv, u_send, u_recv, t_sem, k_sem, i_sem, n_sem,
):
    tile_count = tiles_hbm.shape[0]
    col_tiles = sketch_hbm.shape[0] // R

    def load(src, dst, sem):
        copy = pltpu.make_async_copy(src, dst, sem)
        copy.start()
        return copy

    small = [
        load(src, dst, i_sem.at[i])
        for i, (src, dst) in enumerate([(slots_hbm, slots), (wrow_hbm, wrow), (subsk_hbm, subsk)])
    ]
    per = tile_count // t_sem.shape[0]
    tile_copies = [
        load(tiles_hbm.at[pl.ds(i * per, per)], tiles.at[pl.ds(i * per, per)], t_sem.at[i])
        for i in range(t_sem.shape[0])
    ]
    chunk = sketch_hbm.shape[0] // k_sem.shape[0]

    def load_sketch(first, last):
        for i in range(first, last):
            load(sketch_hbm.at[pl.ds(i * chunk, chunk)], sketch.at[pl.ds(i * chunk, chunk)], k_sem.at[i])

    load_sketch(0, 2)

    slot_pad[...] = jnp.full_like(slot_pad, -1)
    small[0].wait()
    slot_pad[pl.ds(0, 1), pl.ds(0, tile_count)] = slots[...]
    by_tile = jnp.broadcast_to(slot_pad[pl.ds(0, 1), :], (R, slot_pad.shape[1])).T
    which = jnp.minimum(lax.broadcasted_iota(jnp.int32, by_tile.shape, 0), tile_count)
    lane = lax.broadcasted_iota(jnp.int32, by_tile.shape, 1)
    for i in range(index_row.shape[1] // R):
        found = jnp.where(by_tile == lane + i * R, which, tile_count)
        index_row[:, pl.ds(i * R, R)] = jnp.min(found, axis=0, keepdims=True)
    index_copy = load(index_row, index, n_sem)
    tiles[tile_count] = jnp.zeros((R, R), BF)

    row, col = lax.axis_index("row"), lax.axis_index("col")
    position = row * 4 + col
    right, left = (col + 1) % 4, (col + 3) % 4
    across = (col + 2) % 4
    to_right, to_left = (row, right), (row, left)
    chip = row // 2
    core = row - chip * 2
    plane = chip // 4
    x = chip - plane * 4
    x_near = x + 1 - 2 * (x % 2)
    partners = [
        (row, col + 1 - 2 * (col % 2)),
        (row, 3 - col),
        (row + 1 - 2 * core, col),
        ((plane * 4 + x_near) * 2 + core, col),
        ((plane * 4 + 3 - x) * 2 + core, col),
    ]
    upper = [(position // 2**t) % 2 for t in range(LEVELS)]

    barrier = pltpu.get_barrier_semaphore()
    peers = [to_right, to_left] + partners[2:]
    for peer in peers:
        pl.semaphore_signal(barrier, inc=1, device_id=peer, device_id_type=MESH)
    pl.semaphore_wait(barrier, len(peers))

    def remote(src, dst, send, recv, peer):
        return pltpu.make_async_remote_copy(
            src_ref=src, dst_ref=dst, send_sem=send, recv_sem=recv, device_id=peer, device_id_type=MESH
        )

    def rs_copy(parts, n, i):
        src, dst, peer = [
            (parts.at[across, LOW], relay.at[n, 0], to_right),
            (parts.at[across, HIGH], relay.at[n, 1], to_left),
            (parts.at[right, HIGH], fin.at[n, 1], to_right),
            (parts.at[left, LOW], fin.at[n, 2], to_left),
            (staged.at[n, 0], fin.at[n, 0], to_right),
            (staged.at[n, 1], fin.at[n, 3], to_left),
        ][i]
        return remote(src, dst, rs_send.at[n, i], rs_recv.at[n, i], peer)

    def rs_first(parts, n):
        for i in range(4):
            rs_copy(parts, n, i).start()

    def rs_second(parts, n):
        rs_copy(parts, n, 0).wait_recv()
        staged[n, 0] = parts[right, LOW] + relay[n, 0]
        rs_copy(parts, n, 4).start()
        rs_copy(parts, n, 1).wait_recv()
        staged[n, 1] = parts[left, HIGH] + relay[n, 1]
        rs_copy(parts, n, 5).start()

    def rs_last(parts, n, out):
        for i in range(2, 6):
            rs_copy(parts, n, i).wait_recv()
        out[LOW, :] = parts[col, LOW] + (fin[n, 0] + fin[n, 2])
        out[HIGH, :] = parts[col, HIGH] + (fin[n, 1] + fin[n, 3])

    def rs_drain(parts, n):
        for i in range(6):
            rs_copy(parts, n, i).wait_send()

    def ag_copy(buf, n, i, receive=False):
        half = buf.shape[1] // 2
        first, second = pl.ds(0, half), pl.ds(half, half)
        part = [first, second, second, first, first, second][i]
        source = [col, col, col, col, left, right][i]
        target = [left, right, left, right, across, across][i]
        ref = buf.at[target if receive else source, part]
        return remote(ref, ref, ag_send.at[n, i], ag_recv.at[n, i], [to_right, to_left][i % 2])

    def ag_first(buf, n):
        for i in range(4):
            ag_copy(buf, n, i).start()

    def ag_second(buf, n):
        for i in range(2):
            ag_copy(buf, n, i, True).wait_recv()
            ag_copy(buf, n, i + 4).start()
        for i in range(2, 4):
            ag_copy(buf, n, i, True).wait_recv()

    def ag_last(buf, n):
        for i in range(4, 6):
            ag_copy(buf, n, i, True).wait_recv()

    def ag_drain(buf, n):
        for i in range(6):
            ag_copy(buf, n, i).wait_send()

    def pair_copy(buf, base, t, send, recv):
        ref = buf.at[t - base, upper[t]]
        return remote(ref, ref, send.at[t - base], recv.at[t - base], partners[t])

    def pair_wait(buf, base, t, send, recv):
        ref = buf.at[t - base, 1 - upper[t]]
        remote(ref, ref, send.at[t - base], recv.at[t - base], partners[t]).wait_recv()

    def leaf_rows(leaf):
        return pl.ds(pl.multiple_of(leaf * 2 * R, R), 2 * R)

    def block_rows(leaf, first, count):
        return jnp.concatenate(
            [
                jnp.concatenate([tiles[index[0, (2 * leaf + i) * col_tiles + first + k]] for k in range(count)], axis=1)
                for i in range(2)
            ],
            axis=0,
        )

    def partial_samples(leaves, count, arriving):
        for leaf in leaves:
            ybuf[leaf_rows(leaf), :] = jnp.zeros((2 * R, ybuf.shape[1]), F32)

        @pl.loop(0, col_tiles // count)
        def _(p):
            rows = pl.ds(pl.multiple_of(p * count * R, R), count * R)
            if arriving:
                pltpu.make_async_copy(sketch_hbm.at[rows], sketch.at[rows], k_sem.at[p]).wait()
            lhs = jnp.concatenate([block_rows(leaf, p * count, count) for leaf in leaves], axis=0)
            product = dot16(lhs, sketch[rows, :])
            for i, leaf in enumerate(leaves):
                ybuf[leaf_rows(leaf), :] += product[i * 2 * R : (i + 1) * 2 * R]

        for leaf in leaves:
            zparts[leaf] = dot(ybuf[leaf_rows(leaf), :], subsk[...])

    small[1].wait()
    small[2].wait()
    zw[:, HIGH] = dot_bx(wrow[...], subsk[...])
    index_copy.wait()
    for copy in tile_copies:
        copy.wait()
    load_sketch(2, k_sem.shape[0])
    small.append(load(coup_hbm, coup, i_sem.at[3]))
    partial_samples([across, right], col_tiles // k_sem.shape[0], True)
    for i in range(3):
        rs_copy(zparts, 0, i).start()
    partial_samples([left], 16, False)
    rs_copy(zparts, 0, 3).start()
    rs_second(zparts, 0)
    partial_samples([col], 16, False)
    small[3].wait()
    rs_last(zparts, 0, zw.at[:, LOW])

    def share_leaf():
        vbuf[col] = ub[0]
        ag_first(vbuf, 0)
        p0[...] = dot_xb(ub[0], wrow[...], 0, 0)

    def leaf_part(leaf):
        rows = pl.ds(pl.multiple_of(leaf * R, R), R)
        s0[rows, :] = dot3(vbuf[leaf], ybuf[leaf_rows(leaf), :], 0, 0)

    def pair_bases():
        ref = u1.at[upper[1]]
        return remote(ref, ref, u_send, u_recv, partners[1])

    def share_pair():
        u1[upper[1]] = ub[1]
        pair_bases().start()
        ag_second(vbuf, 0)
        leaf_part(col)
        leaf_part(left)
        leaf_part(right)

    def wide_parts():
        def facing(t, other):
            b = coup[t]
            return jnp.where(upper[t] == 1, dot_bx(b, other, 0, 0), dot_bx(b, other))

        def halves(t):
            own = pl.ds(pl.multiple_of(upper[t] * R, R), R)
            other = pl.ds(pl.multiple_of((1 - upper[t]) * R, R), R)
            return ub[t + 1, own, :], ub[t + 1, other, :]

        ag_last(vbuf, 0)
        leaf_part(across)
        own1, other1 = halves(0)
        own2, other2 = halves(1)
        correction = -(dot(facing(0, other1), own2) + dot(own1, facing(1, other2)))
        ref = u1.at[1 - upper[1]]
        remote(ref, ref, u_send, u_recv, partners[1]).wait_recv()
        down[pl.ds(0, 2 * R), :] = dot(u1[0], ub[2, LOW, :])
        down[pl.ds(2 * R, 2 * R), :] = dot(u1[1], ub[2, HIGH, :])
        sample = dot3(down[...], s0[...], 0, 0) + dot3(correction, p0[...], 0, 0)
        proj = dot3(down[pl.ds(pl.multiple_of(col * R, R), R), :], p0[...], 0, 0)
        for k in range(4):
            sparts[k, LOW] = sample[:, k * R : (k + 1) * R]
            sparts[k, HIGH] = proj[:, k * R : (k + 1) * R]
        rs_first(sparts, 1)

    def relay_parts():
        rs_second(sparts, 1)

    def wide_start():
        rs_last(sparts, 1, zw.at[:, LOW])
        comm2[0, upper[2], :, LOW] = zw[LOW, LOW]
        comm2[0, upper[2], :, HIGH] = zw[HIGH, LOW]
        pair_copy(comm2, 2, 2, c2_send, c2_recv).start()
        wide_merge(2)

    def wide_merge(t):
        pair_wait(comm2, 2, t, c2_send, c2_recv)
        low_p, high_p = comm2[t - 2, 0, :, HIGH], comm2[t - 2, 1, :, HIGH]
        pq[LOW, LOW] = comm2[t - 2, 0, :, LOW] - dot_bx(coup[t], high_p)
        pq[HIGH, LOW] = comm2[t - 2, 1, :, LOW] - dot_bx(coup[t], low_p, 0, 0)
        if t == LEVELS - 1:
            topbuf[col] = dot3(ub[t + 1], pq[:, LOW], 0, 0)
            return
        pq[LOW, HIGH] = low_p
        pq[HIGH, HIGH] = high_p
        comm2[t - 1, upper[t + 1]] = dot3(ub[t + 1], pq[...], 0, 0)
        pair_copy(comm2, 2, t + 1, c2_send, c2_recv).start()

    at_middle = {3: relay_parts}
    at_end = {0: share_leaf, 1: share_pair, 2: wide_parts, 3: wide_start, 4: functools.partial(wide_merge, 3)}

    def place(table, t):
        for at, piece in table.items():
            pl.when(t == at)(piece)

    i0 = lax.broadcasted_iota(jnp.int32, (16, 8, R), 0) * 8 + lax.broadcasted_iota(jnp.int32, (16, 8, R), 1)
    eye = i0 == lax.broadcasted_iota(jnp.int32, (16, 8, R), 2)
    one = jnp.broadcast_to(jnp.where(position >= 0, 1.0, 0.0).astype(F32), (8, R))
    pieces = 4
    piece = R // pieces

    def of_level(t, values):
        return sum(jnp.where(t == k, value, 0) for k, value in enumerate(values))

    def stage(t, carry):
        own = of_level(t, upper)
        peer = (of_level(t, [p[0] for p in partners]), of_level(t, [p[1] for p in partners]))
        below = t - 1

        def piece_copy(level, side, i):
            ref = comm.at[level, side, pl.ds(i * piece, piece), :]
            return remote(ref, ref, c_send.at[level, i], c_recv.at[level, i], peer)

        @pl.when(t > 0)
        def _():
            own_below = of_level(below, upper)
            for i in range(pieces):
                piece_copy(below, 1 - own_below, i).wait_recv()
            b = coup[below]
            low_w, high_w = comm[below, 0, :, HIGH], comm[below, 1, :, HIGH]
            zw[LOW, LOW] = comm[below, 0, :, LOW] - dot_bx(b, high_w)
            zw[HIGH, LOW] = comm[below, 1, :, LOW] - dot_bx(b, low_w, 0, 0)
            zw[LOW, HIGH] = low_w
            zw[HIGH, HIGH] = high_w

        z = zw[:, LOW]
        products = dot(z, zw[...], 0, 0)
        gm[...] = products
        shift = 0.0001 * jnp.sum(z * z, keepdims=True) / R + 1e-06
        work[...] = products[:, :R].reshape(16, 8, R) + jnp.where(eye, shift.reshape(1, 1, 1), 0.0)

        def make_piece(i):
            rows = pl.ds(i * piece, piece)
            comm[t, own, rows, :] = dot(linv[rows, :], gm[...])

        def send_piece(i):
            @pl.when(t < LEVELS)
            def _():
                piece_copy(t, own, i).start()

        def segment(j):
            if j == 8:
                place(at_middle, t)
            if j % 4 == 2 and j > 4:
                send_piece(j // 4 - 1)
            if j % 4 == 0 and j > 0:
                make_piece(j // 4 - 1)

        factor(work, linv, one, segment)
        make_piece(pieces - 1)
        send_piece(pieces - 1)
        u = dot(zw[:, LOW], linv[...], 1, 1)
        ub[t] = u

        @pl.when(t == 0)
        def _():
            leaf_out[...] = u

        @pl.when(t > 0)
        def _():
            half = pl.ds(pl.multiple_of(of_level(below, upper) * R, R), R)
            trans_out[below] = ub[t, half, :]

        place(at_end, t)
        return carry

    lax.fori_loop(0, LEVELS + 1, stage, 0)
    wide_merge(LEVELS - 1)
    ag_first(topbuf, 1)
    ag_second(topbuf, 1)
    ag_last(topbuf, 1)
    for k in range(4):
        top_out[:, pl.ds(k * R, R)] = topbuf[k]

    rs_drain(zparts, 0)
    rs_drain(sparts, 1)
    ag_drain(vbuf, 0)
    pair_bases().wait_send()
    ag_drain(topbuf, 1)
    for t in range(LEVELS):
        for i in range(pieces):
            ref = comm.at[t, upper[t], pl.ds(i * piece, piece), :]
            remote(ref, ref, c_send.at[t, i], c_recv.at[t, i], partners[t]).wait_send()
    for t in range(2, LEVELS):
        pair_copy(comm2, 2, t, c2_send, c2_recv).wait_send()


def run_tree(slots, tiles, sketch, wrow, subsketch, couplings):
    vmem = pl.BlockSpec(memory_space=pltpu.VMEM)
    hbm = pl.BlockSpec(memory_space=pltpu.HBM)
    dma = pltpu.SemaphoreType.DMA
    tile_count = tiles.shape[0]
    depth, width = sketch.shape
    slot_count = 8 * depth // R

    def f32(*shape):
        return pltpu.VMEM(shape, F32)

    return pl.pallas_call(
        tree_kernel,
        out_shape=[
            jax.ShapeDtypeStruct((2 * R, R), F32),
            jax.ShapeDtypeStruct((LEVELS, R, R), F32),
            jax.ShapeDtypeStruct((R, width), F32),
        ],
        in_specs=[hbm] * 6,
        out_specs=[vmem, vmem, vmem],
        scratch_shapes=[
            pltpu.VMEM(slots.shape, jnp.int32), pltpu.VMEM((tile_count + 1, R, R), BF), pltpu.VMEM((depth, width), BF), pltpu.VMEM(wrow.shape, BF),
            f32(width, R), pltpu.VMEM(couplings.shape, BF), pltpu.VMEM((1, 2 * R), jnp.int32),
            pltpu.VMEM((1, slot_count), jnp.int32), pltpu.SMEM((1, slot_count), jnp.int32),
            f32(16, 8, R), f32(R, R), f32(R, 2 * R), f32(2 * R, 2 * R), f32(LEVELS + 1, 2 * R, R),
            f32(LEVELS + 1, 2, R, 2 * R), f32(3, 2, R, 2 * R), f32(2, 2, R, R), f32(2, 4, R, R), f32(2, 2, R, R),
            f32(4, 2 * R, R), f32(4, 2 * R, R), f32(4, 2 * R, R), f32(4, R, R), f32(8 * R, width), f32(R, width),
            f32(4 * R, width), f32(2, 2 * R, R), f32(4 * R, R), f32(2 * R, 2 * R),
            dma((2, 6)), dma((2, 6)), dma((2, 6)), dma((2, 6)), dma((LEVELS, 4)), dma((LEVELS, 4)), dma((3,)), dma((3,)), dma, dma,
            dma((4,)), dma((6,)), dma((4,)), dma,
        ],
        compiler_params=pltpu.CompilerParams(
            collective_id=0, has_side_effects=True, vmem_limit_bytes=48 * 2**20
        ),
        name="tree",
    )(*[pltpu.with_memory_space_constraint(a, pltpu.HBM) for a in (slots, tiles, sketch, wrow, subsketch, couplings)])


def store_kernel(*refs):
    copies = [pltpu.make_async_copy(refs[i], refs[i + 3], refs[6].at[i]) for i in range(3)]
    for copy in copies:
        copy.start()
    for copy in copies:
        copy.wait()


def store(*results):
    vmem = pl.BlockSpec(memory_space=pltpu.VMEM)
    hbm = pl.BlockSpec(memory_space=pl.ANY)
    return pl.pallas_call(
        store_kernel,
        out_shape=[jax.ShapeDtypeStruct(a.shape, a.dtype) for a in results],
        in_specs=[vmem] * 3,
        out_specs=[hbm] * 3,
        scratch_shapes=[pltpu.SemaphoreType.DMA((3,))],
        compiler_params=pltpu.CompilerParams(vmem_limit_bytes=2**20),
        name="store",
    )(*results)


def per_device(tiles, tile_slots, sketch, row_sketch, subsketch, couplings):
    leaf_basis, transfer, top = run_tree(
        tile_slots.reshape(1, -1), tiles, sketch, row_sketch, subsketch, couplings[0]
    )
    leaf_basis, transfer, top = store(leaf_basis, transfer, top)
    return leaf_basis, transfer[None], top[None]


def solution(mesh):
    return jax.shard_map(
        per_device,
        mesh=mesh,
        in_specs=(
            P(("row", "col"), None, None),
            P(("row", "col")),
            P("col", None),
            P(("row", "col"), None),
            P(),
            P(("row", "col"), None, None, None),
        ),
        out_specs=(
            P(("row", "col"), None),
            P(("row", "col"), None, None, None),
            P(("row", "col"), None, None),
        ),
        check_vma=False,
    )
```

```python
import functools

import jax
import jax.numpy as jnp
from jax import lax
from jax.experimental import pallas as pl
from jax.experimental.pallas import tpu as pltpu
from jax.sharding import PartitionSpec as P

LEVELS = 5
R = 128
F32 = jnp.float32
BF = jnp.bfloat16
HI = lax.Precision.HIGHEST
MESH = pl.DeviceIdType.MESH
LOW, HIGH = pl.ds(0, R), pl.ds(R, R)


def dot(a, b, ca=1, cb=0):
    return lax.dot_general(a, b, (((ca,), (cb,)), ((), ())), precision=HI, preferred_element_type=F32)


def dot16(a, b, ca=1, cb=0):
    return lax.dot_general(a, b, (((ca,), (cb,)), ((), ())), preferred_element_type=F32)


def split3(x):
    hi = x.astype(BF)
    rest = x - hi.astype(F32)
    mid = rest.astype(BF)
    return hi, mid, (rest - mid.astype(F32)).astype(BF)


def split2(x):
    hi = x.astype(BF)
    return hi, (x - hi.astype(F32)).astype(BF)


def dot3(a, b, ca=1, cb=0):
    a_hi, a_lo = split2(a)
    b_hi, b_lo = split2(b)
    return dot16(a_hi, b_hi, ca, cb) + (dot16(a_hi, b_lo, ca, cb) + dot16(a_lo, b_hi, ca, cb))


def dot6(a, b, ca=1, cb=0):
    a0, a1, a2 = split3(a)
    b0, b1, b2 = split3(b)
    small = dot16(a0, b2, ca, cb) + (dot16(a1, b1, ca, cb) + dot16(a2, b0, ca, cb))
    return dot16(a0, b0, ca, cb) + (dot16(a0, b1, ca, cb) + (dot16(a1, b0, ca, cb) + small))


def dot_bx(b, x, ca=1, cb=0):
    hi, mid, low = split3(x)
    return dot16(b, hi, ca, cb) + (dot16(b, mid, ca, cb) + dot16(b, low, ca, cb))


def dot_xb(x, b, ca=1, cb=0):
    hi, mid, low = split3(x)
    return dot16(hi, b, ca, cb) + (dot16(mid, b, ca, cb) + dot16(low, b, ca, cb))


def row_of(x, k):
    return jnp.broadcast_to(x[k : k + 1, :], x.shape)


def lane_of(x, k):
    return jnp.broadcast_to(x[:, k : k + 1], x.shape)


def factor(t_ref, x_ref, one, segment):
    n = t_ref.shape[0]
    sub = lax.broadcasted_iota(jnp.int32, (8, 128), 0)
    lane = lax.broadcasted_iota(jnp.int32, (8, 128), 1)
    following = t_ref[0]
    cols = [lane_of(following, k) * one for k in range(8)]
    for j in range(n):
        segment(j)
        base = 8 * j
        block = jnp.where(lane == sub + base, 1.0, jnp.where((lane >= base) & (lane < base + 8), 0.0, following))
        rows = [row_of(block, k) for k in range(8)]
        d = [[row_of(cols[k], i) if i >= k else None for k in range(8)] for i in range(8)]
        last = j == n - 1
        if not last:
            nxt = t_ref[j + 1]
            c = [lane_of(nxt, base + k) * one for k in range(8)]
            following = jnp.where((lane >= base) & (lane < base + 8), 0.0, nxt)
            ncols = [lane_of(nxt, base + 8 + k) for k in range(8)]
        inv = []
        mult = [[None] * 8 for _ in range(8)]
        for k in range(8):
            iv = 1.0 / d[k][k]
            inv.append(iv)
            for i in range(k + 1, 8):
                m = d[i][k] * iv
                mult[i][k] = m
                for i2 in range(i, 8):
                    d[i2][i] = d[i2][i] - d[i2][k] * m
                rows[i] = rows[i] - m * rows[k]
                if not last:
                    c[i] = c[i] - m * c[k]
            if not last:
                e = c[k] * iv
                for k2 in range(8):
                    ncols[k2] = ncols[k2] - e * row_of(c[k], k2)
                following = following - e * rows[k]
        out, pivots = rows[0], d[0][0]
        for k in range(1, 8):
            out = jnp.where(sub == k, rows[k], out)
            pivots = jnp.where(sub == k, d[k][k], pivots)
        x_ref[pl.ds(base, 8), :] = jnp.where(lane < base + 8, out * lax.rsqrt(pivots), 0.0)
        if last:
            break
        cols = ncols
        if j < n - 2:
            q = [rows[k] * inv[k] for k in range(8)]
            for k in range(7, 0, -1):
                for i in range(k):
                    q[i] = q[i] - mult[k][i] * q[k]
            for g in range(j + 2, n):
                rest = t_ref[g]
                terms = [lane_of(rest, base + k) * q[k] for k in range(8)]
                while len(terms) > 1:
                    terms = [terms[i] + terms[i + 1] for i in range(0, len(terms), 2)]
                t_ref[g] = jnp.where((lane >= base) & (lane < base + 8), 0.0, rest) - terms[0]


def tree_kernel(
    slots_hbm, tiles_hbm, sketch_hbm, wrow_hbm, subsk_hbm, coup_hbm,
    leaf_out, trans_out, top_out,
    slots, tiles, sketch, wrow, subsk, coup, slot_pad, index_row, index,
    work, linv, gm, zw, ub, comm, comm2, relay, fin, staged, zparts, sparts, vbuf, topbuf, ybuf, p0, s0, u1, down, pq,
    rs_send, rs_recv, ag_send, ag_recv, c_send, c_recv, c2_send, c2_recv, u_send, u_recv, t_sem, k_sem, i_sem, n_sem,
):
    tile_count = tiles_hbm.shape[0]
    col_tiles = sketch_hbm.shape[0] // R

    def load(src, dst, sem):
        copy = pltpu.make_async_copy(src, dst, sem)
        copy.start()
        return copy

    small = [
        load(src, dst, i_sem.at[i])
        for i, (src, dst) in enumerate([(slots_hbm, slots), (wrow_hbm, wrow), (subsk_hbm, subsk)])
    ]
    per = tile_count // t_sem.shape[0]
    tile_copies = [
        load(tiles_hbm.at[pl.ds(i * per, per)], tiles.at[pl.ds(i * per, per)], t_sem.at[i])
        for i in range(t_sem.shape[0])
    ]
    chunk = sketch_hbm.shape[0] // k_sem.shape[0]

    def load_sketch(first, last):
        for i in range(first, last):
            load(sketch_hbm.at[pl.ds(i * chunk, chunk)], sketch.at[pl.ds(i * chunk, chunk)], k_sem.at[i])

    load_sketch(0, 2)

    slot_pad[...] = jnp.full_like(slot_pad, -1)
    small[0].wait()
    slot_pad[pl.ds(0, 1), pl.ds(0, tile_count)] = slots[...]
    by_tile = jnp.broadcast_to(slot_pad[pl.ds(0, 1), :], (R, slot_pad.shape[1])).T
    which = jnp.minimum(lax.broadcasted_iota(jnp.int32, by_tile.shape, 0), tile_count)
    lane = lax.broadcasted_iota(jnp.int32, by_tile.shape, 1)
    for i in range(index_row.shape[1] // R):
        found = jnp.where(by_tile == lane + i * R, which, tile_count)
        index_row[:, pl.ds(i * R, R)] = jnp.min(found, axis=0, keepdims=True)
    index_copy = load(index_row, index, n_sem)
    tiles[tile_count] = jnp.zeros((R, R), BF)

    row, col = lax.axis_index("row"), lax.axis_index("col")
    position = row * 4 + col
    right, left = (col + 1) % 4, (col + 3) % 4
    across = (col + 2) % 4
    to_right, to_left = (row, right), (row, left)
    chip = row // 2
    core = row - chip * 2
    plane = chip // 4
    x = chip - plane * 4
    x_near = x + 1 - 2 * (x % 2)
    partners = [
        (row, col + 1 - 2 * (col % 2)),
        (row, 3 - col),
        (row + 1 - 2 * core, col),
        ((plane * 4 + x_near) * 2 + core, col),
        ((plane * 4 + 3 - x) * 2 + core, col),
    ]
    upper = [(position // 2**t) % 2 for t in range(LEVELS)]

    barrier = pltpu.get_barrier_semaphore()
    peers = [to_right, to_left] + partners[2:]
    for peer in peers:
        pl.semaphore_signal(barrier, inc=1, device_id=peer, device_id_type=MESH)
    pl.semaphore_wait(barrier, len(peers))

    def remote(src, dst, send, recv, peer):
        return pltpu.make_async_remote_copy(
            src_ref=src, dst_ref=dst, send_sem=send, recv_sem=recv, device_id=peer, device_id_type=MESH
        )

    def rs_copy(parts, n, i):
        src, dst, peer = [
            (parts.at[across, LOW], relay.at[n, 0], to_right),
            (parts.at[across, HIGH], relay.at[n, 1], to_left),
            (parts.at[right, HIGH], fin.at[n, 1], to_right),
            (parts.at[left, LOW], fin.at[n, 2], to_left),
            (staged.at[n, 0], fin.at[n, 0], to_right),
            (staged.at[n, 1], fin.at[n, 3], to_left),
        ][i]
        return remote(src, dst, rs_send.at[n, i], rs_recv.at[n, i], peer)

    def rs_first(parts, n):
        for i in range(4):
            rs_copy(parts, n, i).start()

    def rs_second(parts, n):
        rs_copy(parts, n, 0).wait_recv()
        staged[n, 0] = parts[right, LOW] + relay[n, 0]
        rs_copy(parts, n, 4).start()
        rs_copy(parts, n, 1).wait_recv()
        staged[n, 1] = parts[left, HIGH] + relay[n, 1]
        rs_copy(parts, n, 5).start()

    def rs_last(parts, n, out):
        for i in range(2, 6):
            rs_copy(parts, n, i).wait_recv()
        out[LOW, :] = parts[col, LOW] + (fin[n, 0] + fin[n, 2])
        out[HIGH, :] = parts[col, HIGH] + (fin[n, 1] + fin[n, 3])

    def rs_drain(parts, n):
        for i in range(6):
            rs_copy(parts, n, i).wait_send()

    def ag_copy(buf, n, i, receive=False):
        half = buf.shape[1] // 2
        first, second = pl.ds(0, half), pl.ds(half, half)
        part = [first, second, second, first, first, second][i]
        source = [col, col, col, col, left, right][i]
        target = [left, right, left, right, across, across][i]
        ref = buf.at[target if receive else source, part]
        return remote(ref, ref, ag_send.at[n, i], ag_recv.at[n, i], [to_right, to_left][i % 2])

    def ag_first(buf, n):
        for i in range(4):
            ag_copy(buf, n, i).start()

    def ag_second(buf, n):
        for i in range(2):
            ag_copy(buf, n, i, True).wait_recv()
            ag_copy(buf, n, i + 4).start()
        for i in range(2, 4):
            ag_copy(buf, n, i, True).wait_recv()

    def ag_last(buf, n):
        for i in range(4, 6):
            ag_copy(buf, n, i, True).wait_recv()

    def ag_drain(buf, n):
        for i in range(6):
            ag_copy(buf, n, i).wait_send()

    def pair_copy(buf, base, t, send, recv):
        ref = buf.at[t - base, upper[t]]
        return remote(ref, ref, send.at[t - base], recv.at[t - base], partners[t])

    def pair_wait(buf, base, t, send, recv):
        ref = buf.at[t - base, 1 - upper[t]]
        remote(ref, ref, send.at[t - base], recv.at[t - base], partners[t]).wait_recv()

    def leaf_rows(leaf):
        return pl.ds(pl.multiple_of(leaf * 2 * R, R), 2 * R)

    def block_rows(leaf, first, count):
        return jnp.concatenate(
            [
                jnp.concatenate([tiles[index[0, (2 * leaf + i) * col_tiles + first + k]] for k in range(count)], axis=1)
                for i in range(2)
            ],
            axis=0,
        )

    def partial_samples(leaves, count, arriving):
        for leaf in leaves:
            ybuf[leaf_rows(leaf), :] = jnp.zeros((2 * R, ybuf.shape[1]), F32)

        @pl.loop(0, col_tiles // count)
        def _(p):
            rows = pl.ds(pl.multiple_of(p * count * R, R), count * R)
            if arriving:
                pltpu.make_async_copy(sketch_hbm.at[rows], sketch.at[rows], k_sem.at[p]).wait()
            lhs = jnp.concatenate([block_rows(leaf, p * count, count) for leaf in leaves], axis=0)
            product = dot16(lhs, sketch[rows, :])
            for i, leaf in enumerate(leaves):
                ybuf[leaf_rows(leaf), :] += product[i * 2 * R : (i + 1) * 2 * R]

        for leaf in leaves:
            zparts[leaf] = dot6(ybuf[leaf_rows(leaf), :], subsk[...])

    small[1].wait()
    small[2].wait()
    zw[:, HIGH] = dot_bx(wrow[...], subsk[...])
    index_copy.wait()
    for copy in tile_copies:
        copy.wait()
    load_sketch(2, k_sem.shape[0])
    small.append(load(coup_hbm, coup, i_sem.at[3]))
    partial_samples([across, right], col_tiles // k_sem.shape[0], True)
    for i in range(3):
        rs_copy(zparts, 0, i).start()
    partial_samples([left], 16, False)
    rs_copy(zparts, 0, 3).start()
    rs_second(zparts, 0)
    partial_samples([col], 16, False)
    small[3].wait()
    rs_last(zparts, 0, zw.at[:, LOW])

    def share_leaf():
        vbuf[col] = ub[0]
        ag_first(vbuf, 0)
        p0[...] = dot_xb(ub[0], wrow[...], 0, 0)

    def leaf_part(leaf):
        rows = pl.ds(pl.multiple_of(leaf * R, R), R)
        s0[rows, :] = dot3(vbuf[leaf], ybuf[leaf_rows(leaf), :], 0, 0)

    def pair_bases():
        ref = u1.at[upper[1]]
        return remote(ref, ref, u_send, u_recv, partners[1])

    def share_pair():
        u1[upper[1]] = ub[1]
        pair_bases().start()
        ag_second(vbuf, 0)
        leaf_part(col)
        leaf_part(left)
        leaf_part(right)

    def wide_parts():
        def facing(t, other):
            b = coup[t]
            return jnp.where(upper[t] == 1, dot_bx(b, other, 0, 0), dot_bx(b, other))

        def halves(t):
            own = pl.ds(pl.multiple_of(upper[t] * R, R), R)
            other = pl.ds(pl.multiple_of((1 - upper[t]) * R, R), R)
            return ub[t + 1, own, :], ub[t + 1, other, :]

        ag_last(vbuf, 0)
        leaf_part(across)
        own1, other1 = halves(0)
        own2, other2 = halves(1)
        correction = -(dot(facing(0, other1), own2) + dot6(own1, facing(1, other2)))
        ref = u1.at[1 - upper[1]]
        remote(ref, ref, u_send, u_recv, partners[1]).wait_recv()
        down[pl.ds(0, 2 * R), :] = dot6(u1[0], ub[2, LOW, :])
        down[pl.ds(2 * R, 2 * R), :] = dot6(u1[1], ub[2, HIGH, :])
        sample = dot3(down[...], s0[...], 0, 0) + dot3(correction, p0[...], 0, 0)
        proj = dot3(down[pl.ds(pl.multiple_of(col * R, R), R), :], p0[...], 0, 0)
        for k in range(4):
            sparts[k, LOW] = sample[:, k * R : (k + 1) * R]
            sparts[k, HIGH] = proj[:, k * R : (k + 1) * R]
        rs_first(sparts, 1)

    def relay_parts():
        rs_second(sparts, 1)

    def wide_start():
        rs_last(sparts, 1, zw.at[:, LOW])
        comm2[0, upper[2], :, LOW] = zw[LOW, LOW]
        comm2[0, upper[2], :, HIGH] = zw[HIGH, LOW]
        pair_copy(comm2, 2, 2, c2_send, c2_recv).start()

    def wide_merge(t):
        pair_wait(comm2, 2, t, c2_send, c2_recv)
        low_p, high_p = comm2[t - 2, 0, :, HIGH], comm2[t - 2, 1, :, HIGH]
        pq[LOW, LOW] = comm2[t - 2, 0, :, LOW] - dot_bx(coup[t], high_p)
        pq[HIGH, LOW] = comm2[t - 2, 1, :, LOW] - dot_bx(coup[t], low_p, 0, 0)
        if t == LEVELS - 1:
            topbuf[col] = dot3(ub[t + 1], pq[:, LOW], 0, 0)
            return
        pq[LOW, HIGH] = low_p
        pq[HIGH, HIGH] = high_p
        comm2[t - 1, upper[t + 1]] = dot3(ub[t + 1], pq[...], 0, 0)
        pair_copy(comm2, 2, t + 1, c2_send, c2_recv).start()

    at_start = {4: functools.partial(wide_merge, 2)}
    at_middle = {3: relay_parts}
    at_end = {0: share_leaf, 1: share_pair, 2: wide_parts, 3: wide_start, 4: functools.partial(wide_merge, 3)}

    def place(table, t):
        for at, piece in table.items():
            pl.when(t == at)(piece)

    i0 = lax.broadcasted_iota(jnp.int32, (16, 8, R), 0) * 8 + lax.broadcasted_iota(jnp.int32, (16, 8, R), 1)
    eye = i0 == lax.broadcasted_iota(jnp.int32, (16, 8, R), 2)
    one = jnp.broadcast_to(jnp.where(position >= 0, 1.0, 0.0).astype(F32), (8, R))
    pieces = 4
    piece = R // pieces

    def of_level(t, values):
        return sum(jnp.where(t == k, value, 0) for k, value in enumerate(values))

    def stage(t, carry):
        own = of_level(t, upper)
        peer = (of_level(t, [p[0] for p in partners]), of_level(t, [p[1] for p in partners]))
        below = t - 1

        def piece_copy(level, side, i):
            ref = comm.at[level, side, pl.ds(i * piece, piece), :]
            return remote(ref, ref, c_send.at[level, i], c_recv.at[level, i], peer)

        @pl.when(t > 0)
        def _():
            own_below = of_level(below, upper)
            for i in range(pieces):
                piece_copy(below, 1 - own_below, i).wait_recv()
            b = coup[below]
            low_w, high_w = comm[below, 0, :, HIGH], comm[below, 1, :, HIGH]
            zw[LOW, LOW] = comm[below, 0, :, LOW] - dot_bx(b, high_w)
            zw[HIGH, LOW] = comm[below, 1, :, LOW] - dot_bx(b, low_w, 0, 0)
            zw[LOW, HIGH] = low_w
            zw[HIGH, HIGH] = high_w

        place(at_start, t)
        z = zw[:, LOW]
        products = dot6(z, zw[...], 0, 0)
        gm[...] = products
        shift = 0.0001 * jnp.sum(z * z, keepdims=True) / R + 1e-06
        work[...] = products[:, :R].reshape(16, 8, R) + jnp.where(eye, shift.reshape(1, 1, 1), 0.0)

        def make_piece(i):
            rows = pl.ds(i * piece, piece)
            comm[t, own, rows, :] = dot6(linv[rows, :], gm[...])

        def send_piece(i):
            @pl.when(t < LEVELS)
            def _():
                piece_copy(t, own, i).start()

        def segment(j):
            if j == 8:
                place(at_middle, t)
            if j % 4 == 2 and j > 4:
                send_piece(j // 4 - 1)
            if j % 4 == 0 and j > 0:
                make_piece(j // 4 - 1)

        factor(work, linv, one, segment)
        make_piece(pieces - 1)
        send_piece(pieces - 1)
        u = dot6(zw[:, LOW], linv[...], 1, 1)
        ub[t] = u

        @pl.when(t == 0)
        def _():
            leaf_out[...] = u

        @pl.when(t > 0)
        def _():
            half = pl.ds(pl.multiple_of(of_level(below, upper) * R, R), R)
            trans_out[below] = ub[t, half, :]

        place(at_end, t)
        return carry

    lax.fori_loop(0, LEVELS + 1, stage, 0)
    wide_merge(LEVELS - 1)
    ag_first(topbuf, 1)
    ag_second(topbuf, 1)
    ag_last(topbuf, 1)
    for k in range(4):
        top_out[:, pl.ds(k * R, R)] = topbuf[k]

    rs_drain(zparts, 0)
    rs_drain(sparts, 1)
    ag_drain(vbuf, 0)
    pair_bases().wait_send()
    ag_drain(topbuf, 1)
    for t in range(LEVELS):
        for i in range(pieces):
            ref = comm.at[t, upper[t], pl.ds(i * piece, piece), :]
            remote(ref, ref, c_send.at[t, i], c_recv.at[t, i], partners[t]).wait_send()
    for t in range(2, LEVELS):
        pair_copy(comm2, 2, t, c2_send, c2_recv).wait_send()


def run_tree(slots, tiles, sketch, wrow, subsketch, couplings):
    vmem = pl.BlockSpec(memory_space=pltpu.VMEM)
    hbm = pl.BlockSpec(memory_space=pltpu.HBM)
    dma = pltpu.SemaphoreType.DMA
    tile_count = tiles.shape[0]
    depth, width = sketch.shape
    slot_count = 8 * depth // R

    def f32(*shape):
        return pltpu.VMEM(shape, F32)

    return pl.pallas_call(
        tree_kernel,
        out_shape=[
            jax.ShapeDtypeStruct((2 * R, R), F32),
            jax.ShapeDtypeStruct((LEVELS, R, R), F32),
            jax.ShapeDtypeStruct((R, width), F32),
        ],
        in_specs=[hbm] * 6,
        out_specs=[vmem, vmem, vmem],
        scratch_shapes=[
            pltpu.VMEM(slots.shape, jnp.int32), pltpu.VMEM((tile_count + 1, R, R), BF), pltpu.VMEM((depth, width), BF), pltpu.VMEM(wrow.shape, BF),
            f32(width, R), pltpu.VMEM(couplings.shape, BF), pltpu.VMEM((1, 2 * R), jnp.int32),
            pltpu.VMEM((1, slot_count), jnp.int32), pltpu.SMEM((1, slot_count), jnp.int32),
            f32(16, 8, R), f32(R, R), f32(R, 2 * R), f32(2 * R, 2 * R), f32(LEVELS + 1, 2 * R, R),
            f32(LEVELS + 1, 2, R, 2 * R), f32(3, 2, R, 2 * R), f32(2, 2, R, R), f32(2, 4, R, R), f32(2, 2, R, R),
            f32(4, 2 * R, R), f32(4, 2 * R, R), f32(4, 2 * R, R), f32(4, R, R), f32(8 * R, width), f32(R, width),
            f32(4 * R, width), f32(2, 2 * R, R), f32(4 * R, R), f32(2 * R, 2 * R),
            dma((2, 6)), dma((2, 6)), dma((2, 6)), dma((2, 6)), dma((LEVELS, 4)), dma((LEVELS, 4)), dma((3,)), dma((3,)), dma, dma,
            dma((4,)), dma((6,)), dma((4,)), dma,
        ],
        compiler_params=pltpu.CompilerParams(
            collective_id=0, has_side_effects=True, vmem_limit_bytes=48 * 2**20
        ),
        name="tree",
    )(*[pltpu.with_memory_space_constraint(a, pltpu.HBM) for a in (slots, tiles, sketch, wrow, subsketch, couplings)])


def store_kernel(*refs):
    copies = [pltpu.make_async_copy(refs[i], refs[i + 3], refs[6].at[i]) for i in range(3)]
    for copy in copies:
        copy.start()
    for copy in copies:
        copy.wait()


def store(*results):
    vmem = pl.BlockSpec(memory_space=pltpu.VMEM)
    hbm = pl.BlockSpec(memory_space=pl.ANY)
    return pl.pallas_call(
        store_kernel,
        out_shape=[jax.ShapeDtypeStruct(a.shape, a.dtype) for a in results],
        in_specs=[vmem] * 3,
        out_specs=[hbm] * 3,
        scratch_shapes=[pltpu.SemaphoreType.DMA((3,))],
        compiler_params=pltpu.CompilerParams(vmem_limit_bytes=2**20),
        name="store",
    )(*results)


def per_device(tiles, tile_slots, sketch, row_sketch, subsketch, couplings):
    leaf_basis, transfer, top = run_tree(
        tile_slots.reshape(1, -1), tiles, sketch, row_sketch, subsketch, couplings[0]
    )
    leaf_basis, transfer, top = store(leaf_basis, transfer, top)
    return leaf_basis, transfer[None], top[None]


def solution(mesh):
    return jax.shard_map(
        per_device,
        mesh=mesh,
        in_specs=(
            P(("row", "col"), None, None),
            P(("row", "col")),
            P("col", None),
            P(("row", "col"), None),
            P(),
            P(("row", "col"), None, None, None),
        ),
        out_specs=(
            P(("row", "col"), None),
            P(("row", "col"), None, None, None),
            P(("row", "col"), None, None),
        ),
        check_vma=False,
    )
```

```python
import functools

import jax
import jax.numpy as jnp
from jax import lax
from jax.experimental import pallas as pl
from jax.experimental.pallas import tpu as pltpu
from jax.sharding import PartitionSpec as P

LEVELS = 5
R = 128
F32 = jnp.float32
BF = jnp.bfloat16
HI = lax.Precision.HIGHEST
MESH = pl.DeviceIdType.MESH
LOW, HIGH = pl.ds(0, R), pl.ds(R, R)


def dot(a, b, ca=1, cb=0):
    return lax.dot_general(a, b, (((ca,), (cb,)), ((), ())), precision=HI, preferred_element_type=F32)


def dot16(a, b, ca=1, cb=0):
    return lax.dot_general(a, b, (((ca,), (cb,)), ((), ())), preferred_element_type=F32)


def split3(x):
    hi = x.astype(BF)
    rest = x - hi.astype(F32)
    mid = rest.astype(BF)
    return hi, mid, (rest - mid.astype(F32)).astype(BF)


def split2(x):
    hi = x.astype(BF)
    return hi, (x - hi.astype(F32)).astype(BF)


def dot3(a, b, ca=1, cb=0):
    a_hi, a_lo = split2(a)
    b_hi, b_lo = split2(b)
    return dot16(a_hi, b_hi, ca, cb) + (dot16(a_hi, b_lo, ca, cb) + dot16(a_lo, b_hi, ca, cb))


def dot6(a, b, ca=1, cb=0):
    a0, a1, a2 = split3(a)
    b0, b1, b2 = split3(b)
    small = dot16(a0, b2, ca, cb) + (dot16(a1, b1, ca, cb) + dot16(a2, b0, ca, cb))
    return dot16(a0, b0, ca, cb) + (dot16(a0, b1, ca, cb) + (dot16(a1, b0, ca, cb) + small))


def dot_bx(b, x, ca=1, cb=0):
    hi, mid, low = split3(x)
    return dot16(b, hi, ca, cb) + (dot16(b, mid, ca, cb) + dot16(b, low, ca, cb))


def dot_xb(x, b, ca=1, cb=0):
    hi, mid, low = split3(x)
    return dot16(hi, b, ca, cb) + (dot16(mid, b, ca, cb) + dot16(low, b, ca, cb))


def row_of(x, k):
    return jnp.broadcast_to(x[k : k + 1, :], x.shape)


def lane_of(x, k):
    return jnp.broadcast_to(x[:, k : k + 1], x.shape)


def factor(t_ref, x_ref, one, segment):
    n = t_ref.shape[0]
    sub = lax.broadcasted_iota(jnp.int32, (8, 128), 0)
    lane = lax.broadcasted_iota(jnp.int32, (8, 128), 1)
    following = t_ref[0]
    cols = [lane_of(following, k) * one for k in range(8)]
    for j in range(n):
        segment(j)
        base = 8 * j
        block = jnp.where(lane == sub + base, 1.0, jnp.where((lane >= base) & (lane < base + 8), 0.0, following))
        rows = [row_of(block, k) for k in range(8)]
        d = [[row_of(cols[k], i) if i >= k else None for k in range(8)] for i in range(8)]
        last = j == n - 1
        if not last:
            nxt = t_ref[j + 1]
            c = [lane_of(nxt, base + k) * one for k in range(8)]
            following = jnp.where((lane >= base) & (lane < base + 8), 0.0, nxt)
            ncols = [lane_of(nxt, base + 8 + k) for k in range(8)]
        inv = []
        mult = [[None] * 8 for _ in range(8)]
        for k in range(8):
            iv = 1.0 / d[k][k]
            inv.append(iv)
            for i in range(k + 1, 8):
                m = d[i][k] * iv
                mult[i][k] = m
                for i2 in range(i, 8):
                    d[i2][i] = d[i2][i] - d[i2][k] * m
                rows[i] = rows[i] - m * rows[k]
                if not last:
                    c[i] = c[i] - m * c[k]
            if not last:
                e = c[k] * iv
                for k2 in range(8):
                    ncols[k2] = ncols[k2] - e * row_of(c[k], k2)
                following = following - e * rows[k]
        out, pivots = rows[0], d[0][0]
        for k in range(1, 8):
            out = jnp.where(sub == k, rows[k], out)
            pivots = jnp.where(sub == k, d[k][k], pivots)
        x_ref[pl.ds(base, 8), :] = jnp.where(lane < base + 8, out * lax.rsqrt(pivots), 0.0)
        if last:
            break
        cols = ncols
        if j < n - 2:
            q = [rows[k] * inv[k] for k in range(8)]
            for k in range(7, 0, -1):
                for i in range(k):
                    q[i] = q[i] - mult[k][i] * q[k]
            for g in range(j + 2, n):
                rest = t_ref[g]
                terms = [lane_of(rest, base + k) * q[k] for k in range(8)]
                while len(terms) > 1:
                    terms = [terms[i] + terms[i + 1] for i in range(0, len(terms), 2)]
                t_ref[g] = jnp.where((lane >= base) & (lane < base + 8), 0.0, rest) - terms[0]


def tree_kernel(
    slots_hbm, tiles_hbm, sketch_hbm, wrow_hbm, subsk_hbm, coup_hbm,
    leaf_out, trans_out, top_out,
    slots, tiles, sketch, wrow, subsk, coup, slot_pad, index_row, index,
    work, linv, gm, zw, ub, comm, comm2, relay, fin, staged, zparts, sparts, vbuf, topbuf, ybuf, p0, s0, u1, down, pq,
    rs_send, rs_recv, ag_send, ag_recv, c_send, c_recv, c2_send, c2_recv, u_send, u_recv, t_sem, k_sem, i_sem, n_sem,
):
    tile_count = tiles_hbm.shape[0]
    col_tiles = sketch_hbm.shape[0] // R

    def load(src, dst, sem):
        copy = pltpu.make_async_copy(src, dst, sem)
        copy.start()
        return copy

    small = [
        load(src, dst, i_sem.at[i])
        for i, (src, dst) in enumerate([(slots_hbm, slots), (wrow_hbm, wrow), (subsk_hbm, subsk)])
    ]
    per = tile_count // t_sem.shape[0]
    tile_copies = [
        load(tiles_hbm.at[pl.ds(i * per, per)], tiles.at[pl.ds(i * per, per)], t_sem.at[i])
        for i in range(t_sem.shape[0])
    ]
    chunk = sketch_hbm.shape[0] // k_sem.shape[0]

    def load_sketch(first, last):
        for i in range(first, last):
            load(sketch_hbm.at[pl.ds(i * chunk, chunk)], sketch.at[pl.ds(i * chunk, chunk)], k_sem.at[i])

    load_sketch(0, 2)

    slot_pad[...] = jnp.full_like(slot_pad, -1)
    small[0].wait()
    slot_pad[pl.ds(0, 1), pl.ds(0, tile_count)] = slots[...]
    by_tile = jnp.broadcast_to(slot_pad[pl.ds(0, 1), :], (R, slot_pad.shape[1])).T
    which = jnp.minimum(lax.broadcasted_iota(jnp.int32, by_tile.shape, 0), tile_count)
    lane = lax.broadcasted_iota(jnp.int32, by_tile.shape, 1)
    for i in range(index_row.shape[1] // R):
        found = jnp.where(by_tile == lane + i * R, which, tile_count)
        index_row[:, pl.ds(i * R, R)] = jnp.min(found, axis=0, keepdims=True)
    index_copy = load(index_row, index, n_sem)
    tiles[tile_count] = jnp.zeros((R, R), BF)

    row, col = lax.axis_index("row"), lax.axis_index("col")
    position = row * 4 + col
    right, left = (col + 1) % 4, (col + 3) % 4
    across = (col + 2) % 4
    to_right, to_left = (row, right), (row, left)
    chip = row // 2
    core = row - chip * 2
    plane = chip // 4
    x = chip - plane * 4
    x_near = x + 1 - 2 * (x % 2)
    partners = [
        (row, col + 1 - 2 * (col % 2)),
        (row, 3 - col),
        (row + 1 - 2 * core, col),
        ((plane * 4 + x_near) * 2 + core, col),
        ((plane * 4 + 3 - x) * 2 + core, col),
    ]
    upper = [(position // 2**t) % 2 for t in range(LEVELS)]

    barrier = pltpu.get_barrier_semaphore()
    peers = [to_right, to_left] + partners[2:]
    for peer in peers:
        pl.semaphore_signal(barrier, inc=1, device_id=peer, device_id_type=MESH)
    pl.semaphore_wait(barrier, len(peers))

    def remote(src, dst, send, recv, peer):
        return pltpu.make_async_remote_copy(
            src_ref=src, dst_ref=dst, send_sem=send, recv_sem=recv, device_id=peer, device_id_type=MESH
        )

    def rs_copy(parts, n, i):
        src, dst, peer = [
            (parts.at[across, LOW], relay.at[n, 0], to_right),
            (parts.at[across, HIGH], relay.at[n, 1], to_left),
            (parts.at[right, HIGH], fin.at[n, 1], to_right),
            (parts.at[left, LOW], fin.at[n, 2], to_left),
            (staged.at[n, 0], fin.at[n, 0], to_right),
            (staged.at[n, 1], fin.at[n, 3], to_left),
        ][i]
        return remote(src, dst, rs_send.at[n, i], rs_recv.at[n, i], peer)

    def rs_first(parts, n):
        for i in range(4):
            rs_copy(parts, n, i).start()

    def rs_second(parts, n):
        rs_copy(parts, n, 0).wait_recv()
        staged[n, 0] = parts[right, LOW] + relay[n, 0]
        rs_copy(parts, n, 4).start()
        rs_copy(parts, n, 1).wait_recv()
        staged[n, 1] = parts[left, HIGH] + relay[n, 1]
        rs_copy(parts, n, 5).start()

    def rs_last(parts, n, out):
        for i in range(2, 6):
            rs_copy(parts, n, i).wait_recv()
        out[LOW, :] = parts[col, LOW] + (fin[n, 0] + fin[n, 2])
        out[HIGH, :] = parts[col, HIGH] + (fin[n, 1] + fin[n, 3])

    def rs_drain(parts, n):
        for i in range(6):
            rs_copy(parts, n, i).wait_send()

    def ag_copy(buf, n, i, receive=False):
        half = buf.shape[1] // 2
        first, second = pl.ds(0, half), pl.ds(half, half)
        part = [first, second, second, first, first, second][i]
        source = [col, col, col, col, left, right][i]
        target = [left, right, left, right, across, across][i]
        ref = buf.at[target if receive else source, part]
        return remote(ref, ref, ag_send.at[n, i], ag_recv.at[n, i], [to_right, to_left][i % 2])

    def ag_first(buf, n):
        for i in range(4):
            ag_copy(buf, n, i).start()

    def ag_second(buf, n):
        for i in range(2):
            ag_copy(buf, n, i, True).wait_recv()
            ag_copy(buf, n, i + 4).start()
        for i in range(2, 4):
            ag_copy(buf, n, i, True).wait_recv()

    def ag_last(buf, n):
        for i in range(4, 6):
            ag_copy(buf, n, i, True).wait_recv()

    def ag_drain(buf, n):
        for i in range(6):
            ag_copy(buf, n, i).wait_send()

    def pair_copy(buf, base, t, send, recv):
        ref = buf.at[t - base, upper[t]]
        return remote(ref, ref, send.at[t - base], recv.at[t - base], partners[t])

    def pair_wait(buf, base, t, send, recv):
        ref = buf.at[t - base, 1 - upper[t]]
        remote(ref, ref, send.at[t - base], recv.at[t - base], partners[t]).wait_recv()

    def leaf_rows(leaf):
        return pl.ds(pl.multiple_of(leaf * 2 * R, R), 2 * R)

    def block_rows(leaf, first, count):
        return jnp.concatenate(
            [
                jnp.concatenate([tiles[index[0, (2 * leaf + i) * col_tiles + first + k]] for k in range(count)], axis=1)
                for i in range(2)
            ],
            axis=0,
        )

    def partial_samples(leaves, count, arriving):
        def step(start, p, first):
            rows = pl.ds(start, count * R)
            if arriving:
                pltpu.make_async_copy(sketch_hbm.at[rows], sketch.at[rows], k_sem.at[p]).wait()
            lhs = jnp.concatenate([block_rows(leaf, p * count, count) for leaf in leaves], axis=0)
            product = dot16(lhs, sketch[rows, :])
            for i, leaf in enumerate(leaves):
                part = product[i * 2 * R : (i + 1) * 2 * R]
                ybuf[leaf_rows(leaf), :] = part if first else ybuf[leaf_rows(leaf), :] + part

        step(0, 0, True)

        @pl.loop(1, col_tiles // count)
        def _(p):
            step(pl.multiple_of(p * count * R, R), p, False)

        for leaf in leaves:
            zparts[leaf] = dot6(ybuf[leaf_rows(leaf), :], subsk[...])

    small[1].wait()
    small[2].wait()
    zw[:, HIGH] = dot_bx(wrow[...], subsk[...])
    index_copy.wait()
    for copy in tile_copies:
        copy.wait()
    load_sketch(2, k_sem.shape[0])
    small.append(load(coup_hbm, coup, i_sem.at[3]))
    partial_samples([across, right], col_tiles // k_sem.shape[0], True)
    for i in range(3):
        rs_copy(zparts, 0, i).start()
    partial_samples([left], 16, False)
    rs_copy(zparts, 0, 3).start()
    rs_second(zparts, 0)
    partial_samples([col], 16, False)
    small[3].wait()
    rs_last(zparts, 0, zw.at[:, LOW])

    def share_leaf():
        vbuf[col] = ub[0]
        ag_first(vbuf, 0)
        p0[...] = dot_xb(ub[0], wrow[...], 0, 0)

    def leaf_part(leaf):
        rows = pl.ds(pl.multiple_of(leaf * R, R), R)
        s0[rows, :] = dot3(vbuf[leaf], ybuf[leaf_rows(leaf), :], 0, 0)

    def pair_bases():
        ref = u1.at[upper[1]]
        return remote(ref, ref, u_send, u_recv, partners[1])

    def share_pair():
        u1[upper[1]] = ub[1]
        pair_bases().start()
        ag_second(vbuf, 0)
        leaf_part(col)
        leaf_part(left)
        leaf_part(right)

    def wide_parts():
        def facing(t, other):
            b = coup[t]
            return jnp.where(upper[t] == 1, dot_bx(b, other, 0, 0), dot_bx(b, other))

        def halves(t):
            own = pl.ds(pl.multiple_of(upper[t] * R, R), R)
            other = pl.ds(pl.multiple_of((1 - upper[t]) * R, R), R)
            return ub[t + 1, own, :], ub[t + 1, other, :]

        ag_last(vbuf, 0)
        leaf_part(across)
        own1, other1 = halves(0)
        own2, other2 = halves(1)
        correction = -(dot(facing(0, other1), own2) + dot6(own1, facing(1, other2)))
        ref = u1.at[1 - upper[1]]
        remote(ref, ref, u_send, u_recv, partners[1]).wait_recv()
        down[pl.ds(0, 2 * R), :] = dot6(u1[0], ub[2, LOW, :])
        down[pl.ds(2 * R, 2 * R), :] = dot6(u1[1], ub[2, HIGH, :])
        sample = dot3(down[...], s0[...], 0, 0) + dot3(correction, p0[...], 0, 0)
        proj = dot3(down[pl.ds(pl.multiple_of(col * R, R), R), :], p0[...], 0, 0)
        for k in range(4):
            sparts[k, LOW] = sample[:, k * R : (k + 1) * R]
            sparts[k, HIGH] = proj[:, k * R : (k + 1) * R]
        rs_first(sparts, 1)

    def relay_parts():
        rs_second(sparts, 1)

    def wide_start():
        rs_last(sparts, 1, zw.at[:, LOW])
        comm2[0, upper[2], :, LOW] = zw[LOW, LOW]
        comm2[0, upper[2], :, HIGH] = zw[HIGH, LOW]
        pair_copy(comm2, 2, 2, c2_send, c2_recv).start()

    def wide_merge(t):
        pair_wait(comm2, 2, t, c2_send, c2_recv)
        low_p, high_p = comm2[t - 2, 0, :, HIGH], comm2[t - 2, 1, :, HIGH]
        pq[LOW, LOW] = comm2[t - 2, 0, :, LOW] - dot_bx(coup[t], high_p)
        pq[HIGH, LOW] = comm2[t - 2, 1, :, LOW] - dot_bx(coup[t], low_p, 0, 0)
        if t == LEVELS - 1:
            topbuf[col] = dot3(ub[t + 1], pq[:, LOW], 0, 0)
            return
        pq[LOW, HIGH] = low_p
        pq[HIGH, HIGH] = high_p
        comm2[t - 1, upper[t + 1]] = dot3(ub[t + 1], pq[...], 0, 0)
        pair_copy(comm2, 2, t + 1, c2_send, c2_recv).start()

    at_start = {4: functools.partial(wide_merge, 2)}
    at_middle = {3: relay_parts}
    at_end = {0: share_leaf, 1: share_pair, 2: wide_parts, 3: wide_start, 4: functools.partial(wide_merge, 3)}

    def place(table, t):
        for at, piece in table.items():
            pl.when(t == at)(piece)

    i0 = lax.broadcasted_iota(jnp.int32, (16, 8, R), 0) * 8 + lax.broadcasted_iota(jnp.int32, (16, 8, R), 1)
    eye = i0 == lax.broadcasted_iota(jnp.int32, (16, 8, R), 2)
    one = jnp.broadcast_to(jnp.where(position >= 0, 1.0, 0.0).astype(F32), (8, R))
    pieces = 4
    piece = R // pieces

    def of_level(t, values):
        return sum(jnp.where(t == k, value, 0) for k, value in enumerate(values))

    def stage(t, carry):
        own = of_level(t, upper)
        peer = (of_level(t, [p[0] for p in partners]), of_level(t, [p[1] for p in partners]))
        below = t - 1

        def piece_copy(level, side, i):
            ref = comm.at[level, side, pl.ds(i * piece, piece), :]
            return remote(ref, ref, c_send.at[level, i], c_recv.at[level, i], peer)

        @pl.when(t > 0)
        def _():
            own_below = of_level(below, upper)
            for i in range(pieces):
                piece_copy(below, 1 - own_below, i).wait_recv()
            b = coup[below]
            low_w, high_w = comm[below, 0, :, HIGH], comm[below, 1, :, HIGH]
            zw[LOW, LOW] = comm[below, 0, :, LOW] - dot_bx(b, high_w)
            zw[HIGH, LOW] = comm[below, 1, :, LOW] - dot_bx(b, low_w, 0, 0)
            zw[LOW, HIGH] = low_w
            zw[HIGH, HIGH] = high_w

        place(at_start, t)
        z = zw[:, LOW]
        products = dot6(z, zw[...], 0, 0)
        gm[...] = products
        shift = 0.0001 * jnp.sum(z * z, keepdims=True) / R + 1e-06
        work[...] = products[:, :R].reshape(16, 8, R) + jnp.where(eye, shift.reshape(1, 1, 1), 0.0)

        def make_piece(i):
            rows = pl.ds(i * piece, piece)
            comm[t, own, rows, :] = dot6(linv[rows, :], gm[...])

        def send_piece(i):
            @pl.when(t < LEVELS)
            def _():
                piece_copy(t, own, i).start()

        def segment(j):
            if j == 8:
                place(at_middle, t)
            if j % 4 == 2 and j > 4:
                send_piece(j // 4 - 1)
            if j % 4 == 0 and j > 0:
                make_piece(j // 4 - 1)

        factor(work, linv, one, segment)
        make_piece(pieces - 1)
        send_piece(pieces - 1)
        u = dot6(zw[:, LOW], linv[...], 1, 1)
        ub[t] = u

        @pl.when(t == 0)
        def _():
            leaf_out[...] = u

        @pl.when(t > 0)
        def _():
            half = pl.ds(pl.multiple_of(of_level(below, upper) * R, R), R)
            trans_out[below] = ub[t, half, :]

        place(at_end, t)
        return carry

    lax.fori_loop(0, LEVELS + 1, stage, 0)
    wide_merge(LEVELS - 1)
    ag_first(topbuf, 1)
    ag_second(topbuf, 1)
    ag_last(topbuf, 1)
    for k in range(4):
        top_out[:, pl.ds(k * R, R)] = topbuf[k]

    rs_drain(zparts, 0)
    rs_drain(sparts, 1)
    ag_drain(vbuf, 0)
    pair_bases().wait_send()
    ag_drain(topbuf, 1)
    for t in range(LEVELS):
        for i in range(pieces):
            ref = comm.at[t, upper[t], pl.ds(i * piece, piece), :]
            remote(ref, ref, c_send.at[t, i], c_recv.at[t, i], partners[t]).wait_send()
    for t in range(2, LEVELS):
        pair_copy(comm2, 2, t, c2_send, c2_recv).wait_send()


def run_tree(slots, tiles, sketch, wrow, subsketch, couplings):
    vmem = pl.BlockSpec(memory_space=pltpu.VMEM)
    hbm = pl.BlockSpec(memory_space=pltpu.HBM)
    dma = pltpu.SemaphoreType.DMA
    tile_count = tiles.shape[0]
    depth, width = sketch.shape
    slot_count = 8 * depth // R

    def f32(*shape):
        return pltpu.VMEM(shape, F32)

    return pl.pallas_call(
        tree_kernel,
        out_shape=[
            jax.ShapeDtypeStruct((2 * R, R), F32),
            jax.ShapeDtypeStruct((LEVELS, R, R), F32),
            jax.ShapeDtypeStruct((R, width), F32),
        ],
        in_specs=[hbm] * 6,
        out_specs=[vmem, vmem, vmem],
        scratch_shapes=[
            pltpu.VMEM(slots.shape, jnp.int32), pltpu.VMEM((tile_count + 1, R, R), BF), pltpu.VMEM((depth, width), BF), pltpu.VMEM(wrow.shape, BF),
            f32(width, R), pltpu.VMEM(couplings.shape, BF), pltpu.VMEM((1, 2 * R), jnp.int32),
            pltpu.VMEM((1, slot_count), jnp.int32), pltpu.SMEM((1, slot_count), jnp.int32),
            f32(16, 8, R), f32(R, R), f32(R, 2 * R), f32(2 * R, 2 * R), f32(LEVELS + 1, 2 * R, R),
            f32(LEVELS + 1, 2, R, 2 * R), f32(3, 2, R, 2 * R), f32(2, 2, R, R), f32(2, 4, R, R), f32(2, 2, R, R),
            f32(4, 2 * R, R), f32(4, 2 * R, R), f32(4, 2 * R, R), f32(4, R, R), f32(8 * R, width), f32(R, width),
            f32(4 * R, width), f32(2, 2 * R, R), f32(4 * R, R), f32(2 * R, 2 * R),
            dma((2, 6)), dma((2, 6)), dma((2, 6)), dma((2, 6)), dma((LEVELS, 4)), dma((LEVELS, 4)), dma((3,)), dma((3,)), dma, dma,
            dma((4,)), dma((6,)), dma((4,)), dma,
        ],
        compiler_params=pltpu.CompilerParams(
            collective_id=0, has_side_effects=True, vmem_limit_bytes=48 * 2**20
        ),
        name="tree",
    )(*[pltpu.with_memory_space_constraint(a, pltpu.HBM) for a in (slots, tiles, sketch, wrow, subsketch, couplings)])


def store_kernel(*refs):
    copies = [pltpu.make_async_copy(refs[i], refs[i + 3], refs[6].at[i]) for i in range(3)]
    for copy in copies:
        copy.start()
    for copy in copies:
        copy.wait()


def store(*results):
    vmem = pl.BlockSpec(memory_space=pltpu.VMEM)
    hbm = pl.BlockSpec(memory_space=pl.ANY)
    return pl.pallas_call(
        store_kernel,
        out_shape=[jax.ShapeDtypeStruct(a.shape, a.dtype) for a in results],
        in_specs=[vmem] * 3,
        out_specs=[hbm] * 3,
        scratch_shapes=[pltpu.SemaphoreType.DMA((3,))],
        compiler_params=pltpu.CompilerParams(vmem_limit_bytes=2**20),
        name="store",
    )(*results)


def per_device(tiles, tile_slots, sketch, row_sketch, subsketch, couplings):
    leaf_basis, transfer, top = run_tree(
        tile_slots.reshape(1, -1), tiles, sketch, row_sketch, subsketch, couplings[0]
    )
    leaf_basis, transfer, top = store(leaf_basis, transfer, top)
    return leaf_basis, transfer[None], top[None]


def solution(mesh):
    return jax.shard_map(
        per_device,
        mesh=mesh,
        in_specs=(
            P(("row", "col"), None, None),
            P(("row", "col")),
            P("col", None),
            P(("row", "col"), None),
            P(),
            P(("row", "col"), None, None, None),
        ),
        out_specs=(
            P(("row", "col"), None),
            P(("row", "col"), None, None, None),
            P(("row", "col"), None, None),
        ),
        check_vma=False,
    )
```
